32 devices in a mesh: vol: 16 (over z, x, core), slab: 2 (over y).
Axes of the slice: x: 2, y: 2, z: 4, core: 2. Of those that a mesh axis runs over, the one named last changes fastest.
Arguments:
- volumes: bfloat16 [32, 4, 16, 16, 64], P('vol', None, 'slab'), may hold values from -6 to 6
- w_first: bfloat16 [32, 108], replicated, may hold values from -0.625 to 0.625
- w_second: bfloat16 [64, 864], replicated, may hold values from -0.21875 to 0.21875
- w_third: bfloat16 [128, 1728], replicated, may hold values from -0.15625 to 0.15625
- map_grad: bfloat16 [32, 128, 4, 4, 16], P(('vol', 'slab')), may hold values from -6 to 6
Outputs:
- grad_first: float32 [32, 108], replicated
- grad_second: float32 [64, 864], replicated
- grad_third: float32 [128, 1728], replicated
The draws below stay inside these ranges and needn't reach their ends.
All inputs are finite; a program needn't handle non-finite values.
Results may differ from the reference program's by a relative error of at most 0.0071.
Values may be sent and summed in bfloat16 or wider, within the bound.
A program may use at most 64 MiB of HBM per device.

```python
import jax
import jax.numpy as jnp
from jax import lax

C0 = 4
C1 = 32
C2 = 64
C3 = 128
VX = 64
VY = 16
VZ = 16
SAMPLES = 32


def shard_levels(rng, shape, cuts, smallest, top_value):
    loudness = 1.0
    for axis_at, blocks in cuts:
        heights = jax.random.uniform(jax.random.fold_in(jax.random.fold_in(rng, 6), axis_at), (blocks,), jnp.float32, smallest / len(cuts), top_value / len(cuts))
        loudness = loudness * jnp.repeat(jnp.exp(heights), shape[axis_at] // blocks).reshape((-1,) + (1,) * (len(shape) - 1 - axis_at))
    return loudness


def noise(key, dims, width, most, split=(), kind=jnp.bfloat16):
    loudness = shard_levels(key, dims, split, -0.22, 0.18) if split else 1.0
    array = jax.random.normal(key, dims, jnp.float32) * width * loudness
    return jnp.minimum(jnp.maximum(array, -most), most).astype(kind)


def setup_inputs(seed: int = 0) -> dict:
    splits = jax.random.split(jax.random.key(seed), 6)
    volumes = noise(splits[0], (SAMPLES, C0, VZ, VY, VX), 1.0, 6.0, ((0, 16), (2, 2)))
    w_first = noise(splits[1], (C1, 27 * C0), (27 * C0) ** -0.5, 0.625)
    w_second = noise(splits[2], (C2, 27 * C1), (27 * C1) ** -0.5, 0.21875)
    w_third = noise(splits[3], (C3, 27 * C2), (27 * C2) ** -0.5, 0.15625)
    map_grad = noise(splits[4], (SAMPLES, C3, VZ // 4, VY // 4, VX // 4), 1.0, 6.0, ((0, 32),))
    return {"volumes": volumes, "w_first": w_first, "w_second": w_second, "w_third": w_third, "map_grad": map_grad}


FORWARD_DIMS = ('NCDHW', 'OIDHW', 'NCDHW')
FILTER_DIMS = ('CNDHW', 'IODHW', 'CNDHW')
SPREAD_DIMS = ('NCDHW', 'IODHW', 'NCDHW')

def kernel_of(weight):
    channels = weight.shape[1] // 27
    return weight.reshape(weight.shape[0], 3, 3, 3, channels).transpose(0, 4, 1, 2, 3)

def flat_of(kernel):
    return kernel.transpose(0, 2, 3, 4, 1).reshape(kernel.shape[0], -1)

def forward(maps, weight, stride, pads):
    return lax.conv_general_dilated(maps.astype(jnp.float32), kernel_of(weight).astype(jnp.float32), (stride, stride, stride), pads, dimension_numbers=FORWARD_DIMS, precision=lax.Precision.HIGHEST)

def weight_grad(maps, delta, stride, pads):
    bounds = []
    for dim_index in range(3):
        extent = maps.shape[2 + dim_index]
        lower = pads[dim_index][0]
        cells_out = delta.shape[2 + dim_index]
        bounds.append((lower, 3 - extent - lower + (cells_out - 1) * stride))
    kernel = lax.conv_general_dilated(maps.astype(jnp.float32), delta.astype(jnp.float32), (1, 1, 1), bounds, rhs_dilation=(stride, stride, stride), dimension_numbers=FILTER_DIMS, precision=lax.Precision.HIGHEST)
    return flat_of(kernel)

def spread_back(delta, weight, stride):
    kernel = kernel_of(weight)[:, :, ::-1, ::-1, ::-1].astype(jnp.float32)
    return lax.conv_general_dilated(delta.astype(jnp.float32), kernel, (1, 1, 1), ((2, 2), (2, 2), (2, 2)), lhs_dilation=(stride, stride, stride), dimension_numbers=SPREAD_DIMS, precision=lax.Precision.HIGHEST)

def interior(full, shape):
    return full[:, :, 1:1 + shape[2], 1:1 + shape[3], 1:1 + shape[4]]

def silu_slope(pre):
    sigma = jax.nn.sigmoid(pre)
    return sigma * (1.0 + pre * (1.0 - sigma))

def reference(volumes, w_first, w_second, w_third, map_grad):
    full_pads = ((1, 1), (1, 1), (1, 1))

    def one_sample(totals, inputs):
        volume, grad_map = inputs
        volume = volume[None]
        pre_first = forward(volume, w_first, 2, full_pads)
        act_first = jax.nn.silu(pre_first).astype(jnp.bfloat16)
        pre_second = forward(act_first, w_second, 2, full_pads)
        act_second = jax.nn.silu(pre_second).astype(jnp.bfloat16)
        pre_third = forward(act_second, w_third, 1, full_pads)
        delta_third = (grad_map[None].astype(jnp.float32) * silu_slope(pre_third)).astype(jnp.bfloat16)
        step_third = weight_grad(act_second, delta_third, 1, full_pads)
        back_second = interior(spread_back(delta_third, w_third, 1), act_second.shape).astype(jnp.bfloat16)
        delta_second = (back_second.astype(jnp.float32) * silu_slope(pre_second)).astype(jnp.bfloat16)
        step_second = weight_grad(act_first, delta_second, 2, full_pads)
        back_first = interior(spread_back(delta_second, w_second, 2), act_first.shape)
        delta_first = (back_first * silu_slope(pre_first)).astype(jnp.bfloat16)
        step_first = weight_grad(volume, delta_first, 2, full_pads)
        return ((totals[0] + step_first, totals[1] + step_second, totals[2] + step_third), None)
    start = (jnp.zeros((C1, 27 * C0), jnp.float32), jnp.zeros((C2, 27 * C1), jnp.float32), jnp.zeros((C3, 27 * C2), jnp.float32))
    totals, unused = lax.scan(one_sample, start, (volumes, map_grad))
    factor = 1.0 / SAMPLES
    return (totals[0] * factor, totals[1] * factor, totals[2] * factor)
```

```python
import functools

import jax
import jax.numpy as jnp
import numpy as np
from jax import lax
from jax.experimental import pallas as pl
from jax.experimental.pallas import tpu as pltpu
from jax.sharding import PartitionSpec as P

MESH = pl.DeviceIdType.MESH
BLOCK = 8
CHUNKS = 2


def one_hot(rows, cols, pairs):
    table = np.zeros((rows, cols), np.float32)
    for row, col in pairs:
        table[row, col] = 1.0
    return table


def cell_picks(depth, height, stride):
    out_depth, out_height = depth // stride, height // stride
    pairs = []
    for a in range(3):
        for b in range(3):
            for i in range(out_depth):
                for j in range(out_height):
                    z, y = stride * i + a - 1, stride * j + b - 1
                    if 0 <= z < depth and 0 <= y < height:
                        row = ((a * 3 + b) * out_depth + i) * out_height + j
                        pairs.append((row, z * height + y))
    return one_hot(9 * out_depth * out_height, depth * height, pairs)


def tables_of(channels, depth, height, width):
    blocks = width // (2 * BLOCK)
    spread = np.zeros((channels, width, blocks * 128), np.float32)
    for block in range(blocks):
        for at in range(2 * BLOCK + 1):
            x = 2 * BLOCK * block - 1 + at
            if x >= 0:
                for k in range(channels):
                    spread[k, x, block * 128 + at * channels + k] = 1.0
    taps = one_hot(
        27 * channels,
        9 * 128,
        [
            (pair * 3 * channels + lane, pair * 128 + lane)
            for pair in range(9)
            for lane in range(3 * channels)
        ],
    )
    plane, length = (depth // 4) * (height // 4), width // 4
    order = one_hot(
        plane * length,
        plane * length,
        [(l * plane + p, p * length + l) for l in range(length) for p in range(plane)],
    )
    second = cell_picks(depth // 2, height // 2, 2)
    third = cell_picks(depth // 4, height // 4, 1)
    spread = spread.reshape(channels * width, -1)
    tables = (spread, cell_picks(depth, height, 2), second, third, second.T, third.T, taps, order)
    return [jnp.asarray(table, jnp.bfloat16) for table in tables]


def contract(lhs, rhs, rhs_dim=0):
    return lax.dot_general(
        lhs, rhs, (((1,), (rhs_dim,)), ((), ())), preferred_element_type=jnp.float32
    )


def contract_fine(lhs, rhs):
    coarse = half(rhs)
    return contract(lhs, coarse) + contract(lhs, half(rhs - coarse.astype(jnp.float32)))


def sigmoid(pre):
    return 1.0 / (1.0 + jnp.exp(-pre))


def slope_of(pre):
    sigma = sigmoid(pre)
    return sigma * (1.0 + pre * (1.0 - sigma))


def half(value):
    return value.astype(jnp.bfloat16)


def chunk_rows(rows, planes):
    return pl.cdiv(rows, 32 * planes) * 32 * planes


class Load:
    def __init__(self, sources, targets, sems):
        self.copies = [
            pltpu.make_async_copy(source, target, sems.at[index])
            for index, (source, target) in enumerate(zip(sources, targets))
        ]
        self.targets = targets

    def start(self):
        for copy in self.copies:
            copy.start()

    def get(self, index):
        self.copies[index].wait()
        return self.targets[index]


class Exchange:
    def __init__(self, source, held, sems, slabs, ring):
        self.slabs = slabs
        self.source, self.held, self.sems = source, held, sems
        self.vol, self.slab = ring.vol, ring.slab

    def copy(self, step):
        other = lax.rem(self.slab + step, self.slabs)
        return pltpu.make_async_remote_copy(
            src_ref=self.source.at[other],
            dst_ref=self.held.at[self.slab],
            send_sem=self.sems.at[0, step],
            recv_sem=self.sems.at[1, step],
            device_id=(self.vol, other),
            device_id_type=MESH,
        )

    def start(self):
        for step in range(1, self.slabs):
            self.copy(step).start()
        self.held[self.slab] = self.source[self.slab]

    def wait_all(self):
        for step in range(1, self.slabs):
            self.copy(step).wait_recv()

    def drain(self):
        for step in range(1, self.slabs):
            self.copy(step).wait_send()


class Ring:
    def __init__(self, slabs, lines):
        self.slabs, self.lines, self.planes = slabs, lines, 2 * slabs
        self.vol = lax.axis_index("vol")
        self.slab = lax.axis_index("slab")
        self.core = lax.rem(self.vol, 2)
        self.side = lax.rem(self.vol // 2, 2)
        self.at_line = self.vol // 4
        self.at_plane = self.side * slabs + self.slab
        self.half = self.core_of(self.core, self.side, self.at_line)
        self.pair = (self.vol + 1 - 2 * self.core, self.slab)

    def core_of(self, half, side, line):
        return lax.rem(half + side + (2 * line) // self.lines, 2)

    def at(self, line, plane, half):
        side = plane // self.slabs
        core = self.core_of(half, side, line)
        return ((line * 2 + side) * 2 + core, lax.rem(plane, self.slabs))

    def in_plane(self, step, flip=0):
        other = lax.rem(self.at_plane + step, self.planes)
        half = 1 - self.half if flip else self.half
        return other, self.at(self.at_line, other, half)

    def in_line(self, step):
        other = lax.rem(self.at_line + step, self.lines)
        return other, self.at(other, self.at_plane, self.half)

    def greet(self):
        barrier = pltpu.get_barrier_semaphore()
        partners = [self.pair]
        partners += [self.in_plane(step, 0)[1] for step in range(1, self.planes)]
        partners += [self.in_plane(step, 1)[1] for step in range(1, self.planes)]
        partners += [self.in_line(step)[1] for step in range(1, self.lines)]
        for partner in partners:
            pl.semaphore_signal(barrier, inc=1, device_id=partner, device_id_type=MESH)
        return lambda: pl.semaphore_wait(barrier, len(partners))


class Summed:
    def __init__(self, ring, direct, own, from_pair, mine, landed, middle, lined, whole, *sems):
        self.ring, self.direct = ring, direct
        self.own, self.from_pair, self.mine = own, from_pair, mine
        self.landed, self.middle, self.lined = landed, middle, lined
        self.whole = whole
        self.pair_sems, self.plane_sems, self.line_sems = sems
        self.block = middle.shape[0]
        self.rows = ring.planes * self.block
        self.spot = ring.half * ring.planes + ring.at_plane

    def blocks(self, index):
        return pl.ds(pl.multiple_of(index * self.block, 16), self.block)

    def halves(self, index):
        return pl.ds(pl.multiple_of(index * self.rows, 16), self.rows)

    def remote(self, source, target, sems, kind, step, device):
        return pltpu.make_async_remote_copy(
            src_ref=source,
            dst_ref=target,
            send_sem=sems.at[kind, 0, step],
            recv_sem=sems.at[kind, 1, step],
            device_id=device,
            device_id_type=MESH,
        )

    def swap(self):
        return pltpu.make_async_remote_copy(
            src_ref=self.own.at[self.halves(1 - self.ring.half)],
            dst_ref=self.from_pair,
            send_sem=self.pair_sems.at[0],
            recv_sem=self.pair_sems.at[1],
            device_id=self.ring.pair,
            device_id_type=MESH,
        )

    def plane_out(self, step):
        other, device = self.ring.in_plane(step)
        source, target = self.mine.at[self.blocks(other)], self.landed.at[self.blocks(step)]
        return self.remote(source, target, self.plane_sems, 0, step, device)

    def line_out(self, step):
        target = self.lined.at[self.blocks(self.ring.at_line)]
        return self.remote(self.middle, target, self.line_sems, 0, step, self.ring.in_line(step)[1])

    def plane_back(self, step):
        block = self.whole.at[self.blocks(self.spot)]
        return self.remote(block, block, self.plane_sems, 1, step, self.ring.in_plane(step)[1])

    def across(self, step):
        planes = self.ring.planes
        if self.direct:
            source, device = self.ring.at_plane, self.ring.in_plane(step, 1)[1]
        else:
            source, device = lax.rem(self.ring.at_plane - step + planes, planes), self.ring.pair
        block = self.whole.at[self.blocks(self.ring.half * planes + source)]
        return self.remote(block, block, self.plane_sems, 2, step, device)

    def scatter(self):
        self.swap().wait()
        own = self.own[self.halves(self.ring.half), :].astype(jnp.float32)
        self.mine[...] = half(own + self.from_pair[...].astype(jnp.float32))
        for step in range(1, self.ring.planes):
            self.plane_out(step).start()

    def gather_plane(self):
        running = self.mine[self.blocks(self.ring.at_plane), :].astype(jnp.float32)
        for step in range(1, self.ring.planes):
            self.plane_out(step).wait_recv()
            running = running + self.landed[self.blocks(step), :].astype(jnp.float32)
        self.middle[...] = half(running)
        for step in range(1, self.ring.lines):
            self.line_out(step).start()

    def gather_line(self):
        self.lined[self.blocks(self.ring.at_line), :] = self.middle[...]
        for step in range(1, self.ring.lines):
            self.line_out(step).wait_recv()
        running = self.lined[: self.block, :].astype(jnp.float32)
        for index in range(1, self.ring.lines):
            running = running + self.lined[self.blocks(index), :].astype(jnp.float32)
        self.whole[self.blocks(self.spot), :] = half(running)

    def spread(self):
        for step in range(1, self.ring.planes):
            self.plane_back(step).start()
            if self.direct:
                self.across(step).start()
        self.across(0).start()

    def pass_on(self):
        for step in range(1, self.ring.planes):
            self.plane_back(step).wait_recv()
            if not self.direct:
                self.across(step).start()

    def settle(self):
        for step in range(self.ring.planes):
            self.across(step).wait_recv()

    def drain(self):
        for step in range(self.ring.planes):
            self.across(step).wait_send()
        for step in range(1, self.ring.planes):
            self.plane_out(step).wait_send()
            self.plane_back(step).wait_send()
        for step in range(1, self.ring.lines):
            self.line_out(step).wait_send()


def step_kernel(slabs, lines, chunks, factor, *refs):
    sources, refs = refs[:13], refs[13:]
    (first_out, second_out, third_out), refs = refs[:3], refs[3:]
    loaded, load_sems, refs = refs[:13], refs[13], refs[14:]
    (p1, p2, p3, w1b, w2p, w3p, a2, even3, odd3, even2, odd2, rows2, g2), refs = refs[:13], refs[13:]
    outgoing, vol, vol_sems, late_own, early_own, *parts = refs
    ring = Ring(slabs, lines)
    ready = ring.greet()
    load = Load(sources, loaded, load_sems)
    load.start()
    late_rows = late_own.shape[0] // chunks
    late = [
        Summed(ring, False, late_own.at[pl.ds(at * late_rows, late_rows)], *parts[9 * at : 9 * at + 9])
        for at in range(chunks)
    ]
    early = Summed(ring, True, early_own, *parts[9 * chunks :])

    raw = load.get(0)
    for part in range(slabs):
        outgoing[part] = jnp.concatenate([raw[part, k] for k in range(raw.shape[1])], axis=1)
    ready()
    incoming = Exchange(outgoing, vol, vol_sems, slabs, ring)
    incoming.start()

    f32 = jnp.float32
    channels = raw.shape[1]
    w1, w2, w3, mg = load.get(1), load.get(2), load.get(3), load.get(4)
    spread, pick1, pick2, pick3, back2, back3, taps, order = [load.get(at) for at in range(5, 13)]
    c1, c2, c3 = w1.shape[0], w2.shape[0], w3.shape[1]
    blocks = spread.shape[1] // 128
    plane1, plane2 = pick1.shape[0] // 9, pick2.shape[0] // 9
    length2 = mg.shape[0] // plane2
    width1 = blocks * BLOCK * c1
    width2 = length2 * c2

    wide = contract(w1[...], taps[...])
    for pair in range(9):
        tile = wide[:, pair * 128 : (pair + 1) * 128]
        for l in range(BLOCK):
            moved = pltpu.roll(tile, 2 * l * channels, 1) if l else tile
            w1b[l * c1 : (l + 1) * c1, pair * 128 : (pair + 1) * 128] = half(moved)
    w2p[...] = jnp.zeros_like(w2p)
    w3p[...] = jnp.zeros_like(w3p)
    for pair in range(9):
        w2p[:, pair * 128 : pair * 128 + 3 * c1] = w2[:, pair * 3 * c1 : (pair + 1) * 3 * c1]
        w3p[pair * 256 : pair * 256 + 3 * c2, :] = w3[pair * 3 * c2 : (pair + 1) * 3 * c2, :]

    given = contract(order[...], mg[...])
    late_own[27 * c2 :, :] = jnp.zeros((late_own.shape[0] - 27 * c2, c3), jnp.bfloat16)
    early_own[...] = jnp.zeros_like(early_own)
    incoming.wait_all()
    levels = [half(contract(vol[part], spread[...])) for part in range(slabs)]
    r1 = half(contract(pick1[...], jnp.concatenate(levels, axis=0)))
    for pair in range(9):
        for block in range(blocks):
            p1[block * plane1 : (block + 1) * plane1, pair * 128 : (pair + 1) * 128] = r1[
                pair * plane1 : (pair + 1) * plane1, block * 128 : (block + 1) * 128
            ]
    pre1 = contract(p1[...], w1b[...], 1)
    act1 = half(pre1 * sigmoid(pre1))
    a1 = jnp.concatenate(
        [act1[block * plane1 : (block + 1) * plane1, :] for block in range(blocks)], axis=1
    )
    r2 = contract(pick2[...], a1)
    r2 = jnp.concatenate([r2, jnp.zeros((9 * plane2, 128), f32)], axis=1)
    sides = (half(pltpu.roll(r2, c1, 1)), half(pltpu.roll(r2, width1 + 128 - c1, 1)))
    for l in range(length2):
        chunk = sides[l % 2][:, (l // 2) * 128 : (l // 2 + 1) * 128]
        for pair in range(9):
            p2[l * plane2 : (l + 1) * plane2, pair * 128 : (pair + 1) * 128] = chunk[
                pair * plane2 : (pair + 1) * plane2, :
            ]
    pre2 = contract(p2[...], w2p[...], 1)
    act2 = pre2 * sigmoid(pre2)
    for l in range(length2):
        a2[:, l * c2 : (l + 1) * c2] = act2[l * plane2 : (l + 1) * plane2, :]
    r3 = contract(pick3[...], half(a2[...]))
    r3 = jnp.concatenate([r3, jnp.zeros((9 * plane2, 256), f32)], axis=1)
    sides = (half(pltpu.roll(r3, c2, 1)), half(r3))
    for l in range(length2):
        chunk = sides[l % 2][:, (l // 2) * 128 : (l // 2) * 128 + 256]
        for pair in range(9):
            p3[l * plane2 : (l + 1) * plane2, pair * 256 : (pair + 1) * 256] = chunk[
                pair * plane2 : (pair + 1) * plane2, :
            ]
    pre3 = contract(p3[...], w3p[...])
    slope3 = given * slope_of(pre3)
    delta3 = half(slope3)
    grad3 = contract(half(slope3.T), p3[...])
    for pair in range(9):
        for lane in range(0, 3 * c2, 128):
            wide = min(128, 3 * c2 - lane)
            turned = grad3[:, pair * 256 + lane : pair * 256 + lane + 128].T
            at = pair * 3 * c2 + lane
            late_own[at : at + wide, :] = half(turned[:wide, :])
    for chunk in late:
        chunk.swap().start()

    spread3 = contract(delta3, w3p[...], 1)
    for pair in range(9):
        for side, holder in ((0, even3), (1, odd3)):
            for tile in range(length2 // 2 + 1):
                total = None
                for part in range(2):
                    l = 2 * (tile - part) + side
                    if 0 <= l < length2:
                        piece = spread3[
                            l * plane2 : (l + 1) * plane2,
                            pair * 256 + part * 128 : pair * 256 + part * 128 + 128,
                        ]
                        total = piece if total is None else total + piece
                holder[pair * plane2 : (pair + 1) * plane2, tile * 128 : (tile + 1) * 128] = total
    down = contract_fine(back3[...], even3[...])
    down = pltpu.roll(down, down.shape[1] - c2, 1) + contract_fine(back3[...], odd3[...])
    for l in range(length2):
        rows2[l * plane2 : (l + 1) * plane2, :] = down[:, l * c2 : (l + 1) * c2]
    slope2 = half(rows2[...]).astype(f32) * slope_of(pre2)
    delta2 = half(slope2)
    for chunk in late:
        chunk.scatter()
    grad2 = contract(half(slope2.T), p2[...])
    g2[...] = jnp.zeros_like(g2)
    for pair in range(9):
        g2[:, pair * 3 * c1 : (pair + 1) * 3 * c1] = grad2[:, pair * 128 : pair * 128 + 3 * c1]

    spread2 = contract(delta2, w2p[...])
    for pair in range(9):
        for l in range(length2):
            holder = odd2 if l % 2 else even2
            holder[pair * plane2 : (pair + 1) * plane2, (l // 2) * 128 : (l // 2 + 1) * 128] = spread2[
                l * plane2 : (l + 1) * plane2, pair * 128 : (pair + 1) * 128
            ]
    tail = jnp.zeros((plane1, 128), f32)
    left = jnp.concatenate([contract_fine(back2[...], even2[...]), tail], axis=1)
    right = jnp.concatenate([contract_fine(back2[...], odd2[...]), tail], axis=1)
    down = pltpu.roll(left, width1 + 128 - c1, 1) + pltpu.roll(right, c1, 1)
    step = BLOCK * c1
    down = jnp.concatenate([down[:, block * step : (block + 1) * step] for block in range(blocks)], axis=0)
    slope1 = down * slope_of(pre1)
    grad1 = contract(half(slope1.T), p1[...])
    tiles = []
    for pair in range(9):
        total = grad1[:c1, pair * 128 : (pair + 1) * 128]
        for l in range(1, BLOCK):
            tile = grad1[l * c1 : (l + 1) * c1, pair * 128 : (pair + 1) * 128]
            total = total + pltpu.roll(tile, 128 - 2 * l * channels, 1)
        tiles.append(half(total))
    first = contract(jnp.concatenate(tiles, axis=1), taps[...], 1)

    tiles2 = g2.shape[1] // 128
    for tile in range(tiles2):
        early_own[tile * c2 : (tile + 1) * c2, :] = half(g2[:, tile * 128 : (tile + 1) * 128])
    early_own[tiles2 * c2 : tiles2 * c2 + c1, : first.shape[1]] = half(first)
    early.swap().start()
    late[0].gather_plane()
    early.scatter()
    for chunk in late[1:]:
        chunk.gather_plane()
    early.gather_plane()
    for chunk in late:
        chunk.gather_line()
        chunk.spread()
    early.gather_line()
    early.spread()
    for chunk in late:
        chunk.pass_on()
    for at, chunk in enumerate(late):
        chunk.settle()
        low, high = at * late_rows, min(27 * c2, (at + 1) * late_rows)
        third_out[low:high, :] = chunk.whole[: high - low, :].astype(f32) * factor
    early.pass_on()
    early.settle()
    for tile in range(tiles2):
        wide = min(128, second_out.shape[1] - tile * 128)
        value = early.whole[tile * c2 : (tile + 1) * c2, :].astype(f32) * factor
        second_out[:, tile * 128 : tile * 128 + wide] = value[:, :wide]
    value = early.whole[tiles2 * c2 : tiles2 * c2 + c1, :].astype(f32) * factor
    first_out[...] = value[:, : first_out.shape[1]]
    for part in (*late, early, incoming):
        part.drain()


def per_device(volumes, w_first, w_second, w_third, map_grad):
    slabs = lax.axis_size("slab")
    devices = lax.axis_size("vol") * slabs
    chips = devices // 2
    lines = chips // (2 * slabs)
    factor = 1.0 / (map_grad.shape[0] * devices)
    parts, channels, level, height, width = volumes.shape
    depth = level * slabs
    tables = tables_of(channels, depth, height, width)
    c1, c2, c3 = w_first.shape[0], w_second.shape[0], w_third.shape[0]
    plane1 = depth * height // 4
    plane2 = depth * height // 16
    length2 = width // 4
    cells = plane2 * length2
    bf16, f32 = jnp.bfloat16, jnp.float32
    planes, chunks = 2 * slabs, CHUNKS
    tiles2 = pl.cdiv(27 * c1, 128)
    late_rows = chunk_rows(pl.cdiv(27 * c2, chunks), planes)
    early_rows = chunk_rows(tiles2 * c2 + c1, planes)
    operands = (
        volumes.reshape(parts, channels, level * height, width),
        w_first,
        w_second,
        w_third.T,
        map_grad[0].transpose(1, 2, 3, 0).reshape(cells, c3),
        *tables,
    )
    dma = pltpu.SemaphoreType.DMA
    scratch = [(operand.shape, operand.dtype) for operand in operands]
    scratch.append(dma((len(operands),)))
    scratch += [
        ((width // (2 * BLOCK) * plane1, 9 * 128), bf16),
        ((cells, 9 * 128), bf16),
        ((cells, 9 * 256), bf16),
        ((BLOCK * c1, 9 * 128), bf16),
        ((c2, 9 * 128), bf16),
        ((9 * 256, c3), bf16),
        ((plane2, length2 * c2), f32),
        ((9 * plane2, length2 * c2 + 128), f32),
        ((9 * plane2, length2 * c2 + 128), f32),
        ((9 * plane2, width // 2 * c1), f32),
        ((9 * plane2, width // 2 * c1), f32),
        ((cells, c2), f32),
        ((c2, tiles2 * 128), f32),
        ((slabs, level * height, channels * width), bf16),
        ((slabs, level * height, channels * width), bf16),
        dma((2, slabs)),
        ((chunks * late_rows, c3), bf16),
        ((early_rows, 128), bf16),
    ]
    for rows in [late_rows] * chunks + [early_rows]:
        block = rows // (2 * planes)
        for count in (planes, planes, planes, 1, lines, 2 * planes):
            scratch.append(((count * block, 128), bf16))
        scratch += [dma((2,)), dma((3, 2, planes)), dma((1, 2, lines))]
    scratch = [pltpu.VMEM(*entry) if isinstance(entry, tuple) else entry for entry in scratch]
    in_hbm = pl.BlockSpec(memory_space=pltpu.HBM)
    in_vmem = pl.BlockSpec(memory_space=pltpu.VMEM)
    first, second, third = pl.pallas_call(
        functools.partial(step_kernel, slabs, lines, chunks, factor),
        out_shape=[
            pltpu.VMEM(shape, f32) for shape in (w_first.shape, w_second.shape, (27 * c2, c3))
        ],
        in_specs=[in_hbm] * len(operands),
        out_specs=[in_vmem] * 3,
        scratch_shapes=scratch,
        compiler_params=pltpu.CompilerParams(
            collective_id=0, has_side_effects=True, vmem_limit_bytes=(56) << 20
        ),
        name="step",
    )(*operands)
    return first, second, third.T


def solution(mesh):
    return jax.shard_map(
        per_device,
        mesh=mesh,
        in_specs=(
            P("vol", None, "slab", None, None),
            P(),
            P(),
            P(),
            P(("vol", "slab"), None, None, None, None),
        ),
        out_specs=(P(), P(), P()),
        check_vma=False,
    )
```

```python
import functools

import jax
import jax.numpy as jnp
import numpy as np
from jax import lax
from jax.experimental import pallas as pl
from jax.experimental.pallas import tpu as pltpu
from jax.sharding import PartitionSpec as P

MESH = pl.DeviceIdType.MESH
BLOCK = 8
SHARES = (7, 7)
DIRECT = ((True, False), (False, False), (True, True))
SPLITS = (1, 2, 4)


def one_hot(rows, cols, pairs):
    table = np.zeros((rows, cols), np.float32)
    for row, col in pairs:
        table[row, col] = 1.0
    return table


def cell_picks(depth, height, stride):
    out_depth, out_height = depth // stride, height // stride
    pairs = []
    for a in range(3):
        for b in range(3):
            for i in range(out_depth):
                for j in range(out_height):
                    z, y = stride * i + a - 1, stride * j + b - 1
                    if 0 <= z < depth and 0 <= y < height:
                        row = ((a * 3 + b) * out_depth + i) * out_height + j
                        pairs.append((row, z * height + y))
    return one_hot(9 * out_depth * out_height, depth * height, pairs)


def tables_of(channels, depth, height, width):
    blocks = width // (2 * BLOCK)
    spread = np.zeros((channels, width, blocks * 128), np.float32)
    for block in range(blocks):
        for at in range(2 * BLOCK + 1):
            x = 2 * BLOCK * block - 1 + at
            if x >= 0:
                for k in range(channels):
                    spread[k, x, block * 128 + at * channels + k] = 1.0
    taps = one_hot(
        27 * channels,
        9 * 128,
        [
            (pair * 3 * channels + lane, pair * 128 + lane)
            for pair in range(9)
            for lane in range(3 * channels)
        ],
    )
    plane, length = (depth // 4) * (height // 4), width // 4
    order = one_hot(
        plane * length,
        plane * length,
        [(l * plane + p, p * length + l) for l in range(length) for p in range(plane)],
    )
    second = cell_picks(depth // 2, height // 2, 2)
    third = cell_picks(depth // 4, height // 4, 1)
    spread = spread.reshape(channels * width, -1)
    tables = (spread, cell_picks(depth, height, 2), second, third, second.T, third.T, taps, order)
    return [jnp.asarray(table, jnp.bfloat16) for table in tables]


def contract(lhs, rhs, rhs_dim=0):
    return lax.dot_general(
        lhs, rhs, (((1,), (rhs_dim,)), ((), ())), preferred_element_type=jnp.float32
    )


def contract_fine(lhs, rhs):
    coarse = half(rhs)
    return contract(lhs, coarse) + contract(lhs, half(rhs - coarse.astype(jnp.float32)))


def sigmoid(pre):
    return 1.0 / (1.0 + jnp.exp(-pre))


def slope_of(pre):
    sigma = sigmoid(pre)
    return sigma * (1.0 + pre * (1.0 - sigma))


def half(value):
    return value.astype(jnp.bfloat16)


def chunk_rows(rows, planes):
    return pl.cdiv(rows, 32 * planes) * 32 * planes


def cuts_of(rows, planes, shares):
    units = chunk_rows(rows, planes) // (32 * planes)
    bounds = [units * sum(shares[:at]) // sum(shares) for at in range(len(shares) + 1)]
    return [32 * planes * (high - low) for low, high in zip(bounds, bounds[1:]) if high > low]


class Load:
    def __init__(self, sources, targets, sems):
        self.copies = [
            pltpu.make_async_copy(source, target, sems.at[index])
            for index, (source, target) in enumerate(zip(sources, targets))
        ]
        self.targets = targets

    def start(self):
        for copy in self.copies:
            copy.start()

    def get(self, index):
        self.copies[index].wait()
        return self.targets[index]


class Exchange:
    def __init__(self, source, held, sems, slabs, ring):
        self.slabs = slabs
        self.source, self.held, self.sems = source, held, sems
        self.vol, self.slab = ring.vol, ring.slab

    def copy(self, step):
        other = lax.rem(self.slab + step, self.slabs)
        return pltpu.make_async_remote_copy(
            src_ref=self.source.at[other],
            dst_ref=self.held.at[self.slab],
            send_sem=self.sems.at[0, step],
            recv_sem=self.sems.at[1, step],
            device_id=(self.vol, other),
            device_id_type=MESH,
        )

    def start(self):
        for step in range(1, self.slabs):
            self.copy(step).start()
        self.held[self.slab] = self.source[self.slab]

    def wait_all(self):
        for step in range(1, self.slabs):
            self.copy(step).wait_recv()

    def drain(self):
        for step in range(1, self.slabs):
            self.copy(step).wait_send()


class Ring:
    def __init__(self, slabs, lines):
        self.slabs, self.lines, self.planes = slabs, lines, 2 * slabs
        self.vol = lax.axis_index("vol")
        self.slab = lax.axis_index("slab")
        self.core = lax.rem(self.vol, 2)
        self.side = lax.rem(self.vol // 2, 2)
        self.at_line = self.vol // 4
        self.at_plane = self.side * slabs + self.slab
        self.half = self.core_of(self.core, self.side, self.at_line)
        self.pair = (self.vol + 1 - 2 * self.core, self.slab)

    def core_of(self, half, side, line):
        return half

    def at(self, line, plane, half):
        side = plane // self.slabs
        core = self.core_of(half, side, line)
        return ((line * 2 + side) * 2 + core, lax.rem(plane, self.slabs))

    def in_plane(self, step, flip=0):
        other = lax.rem(self.at_plane + step, self.planes)
        half = 1 - self.half if flip else self.half
        return other, self.at(self.at_line, other, half)

    def in_line(self, step):
        other = lax.rem(self.at_line + step, self.lines)
        return other, self.at(other, self.at_plane, self.half)

    def greet(self):
        barrier = pltpu.get_barrier_semaphore()
        partners = [self.pair]
        partners += [self.in_plane(step, 0)[1] for step in range(1, self.planes)]
        partners += [self.in_plane(step, 1)[1] for step in range(1, self.planes)]
        partners += [self.in_line(step)[1] for step in range(1, self.lines)]
        for partner in partners:
            pl.semaphore_signal(barrier, inc=1, device_id=partner, device_id_type=MESH)
        return lambda: pl.semaphore_wait(barrier, len(partners))


class Summed:
    def __init__(self, ring, direct_out, direct, own, from_pair, mine, landed, middle, lined, whole, *sems):
        self.ring, self.direct_out, self.direct = ring, direct_out, direct
        self.own, self.from_pair, self.mine = own, from_pair, mine
        self.landed, self.middle, self.lined = landed, middle, lined
        self.whole = whole
        self.pair_sems, self.plane_sems, self.line_sems = sems
        self.block = middle.shape[0]
        self.rows = ring.planes * self.block
        self.spot = ring.half * ring.planes + ring.at_plane

    def blocks(self, index):
        return pl.ds(pl.multiple_of(index * self.block, 16), self.block)

    def halves(self, index):
        return pl.ds(pl.multiple_of(index * self.rows, 16), self.rows)

    def remote(self, source, target, sems, kind, step, device):
        return pltpu.make_async_remote_copy(
            src_ref=source,
            dst_ref=target,
            send_sem=sems.at[kind, 0, step],
            recv_sem=sems.at[kind, 1, step],
            device_id=device,
            device_id_type=MESH,
        )

    def swap(self):
        return pltpu.make_async_remote_copy(
            src_ref=self.own.at[self.halves(1 - self.ring.half)],
            dst_ref=self.from_pair,
            send_sem=self.pair_sems.at[0],
            recv_sem=self.pair_sems.at[1],
            device_id=self.ring.pair,
            device_id_type=MESH,
        )

    def plane_out(self, step, flip=0):
        other, device = self.ring.in_plane(step, flip)
        target = self.landed.at[self.blocks(flip * self.ring.planes + step)]
        if self.direct_out:
            half_at = 1 - self.ring.half if flip else self.ring.half
            source = self.own.at[self.blocks(half_at * self.ring.planes + other)]
        else:
            source = self.mine.at[self.blocks(other)]
        return self.remote(source, target, self.plane_sems, 3 * flip, step, device)

    def outs(self):
        steps = [(step, 0) for step in range(1, self.ring.planes)]
        if self.direct_out:
            steps += [(step, 1) for step in range(self.ring.planes)]
        return steps

    def line_out(self, step):
        target = self.lined.at[self.blocks(self.ring.at_line)]
        return self.remote(self.middle, target, self.line_sems, 0, step, self.ring.in_line(step)[1])

    def plane_back(self, step):
        block = self.whole.at[self.blocks(self.spot)]
        return self.remote(block, block, self.plane_sems, 1, step, self.ring.in_plane(step)[1])

    def across(self, step):
        planes = self.ring.planes
        if self.direct:
            source, device = self.ring.at_plane, self.ring.in_plane(step, 1)[1]
        else:
            source, device = lax.rem(self.ring.at_plane - step + planes, planes), self.ring.pair
        block = self.whole.at[self.blocks(self.ring.half * planes + source)]
        return self.remote(block, block, self.plane_sems, 2, step, device)

    def begin(self):
        if self.direct_out:
            for step, flip in self.outs():
                self.plane_out(step, flip).start()
        else:
            self.swap().start()

    def scatter(self):
        if self.direct_out:
            return
        self.swap().wait()
        own = self.own[self.halves(self.ring.half), :].astype(jnp.float32)
        self.mine[...] = half(own + self.from_pair[...].astype(jnp.float32))
        for step, flip in self.outs():
            self.plane_out(step, flip).start()

    def gather_plane(self):
        if self.direct_out:
            running = self.own[self.blocks(self.spot), :].astype(jnp.float32)
        else:
            running = self.mine[self.blocks(self.ring.at_plane), :].astype(jnp.float32)
        for step, flip in self.outs():
            self.plane_out(step, flip).wait_recv()
            slot = self.blocks(flip * self.ring.planes + step)
            running = running + self.landed[slot, :].astype(jnp.float32)
        self.middle[...] = half(running)
        for step in range(1, self.ring.lines):
            self.line_out(step).start()

    def gather_line(self):
        self.lined[self.blocks(self.ring.at_line), :] = self.middle[...]
        for step in range(1, self.ring.lines):
            self.line_out(step).wait_recv()
        running = self.lined[: self.block, :].astype(jnp.float32)
        for index in range(1, self.ring.lines):
            running = running + self.lined[self.blocks(index), :].astype(jnp.float32)
        self.whole[self.blocks(self.spot), :] = half(running)

    def spread(self):
        for step in range(1, self.ring.planes):
            self.plane_back(step).start()
            if self.direct:
                self.across(step).start()
        self.across(0).start()

    def pass_on(self):
        for step in range(1, self.ring.planes):
            self.plane_back(step).wait_recv()
            if not self.direct:
                self.across(step).start()

    def settle(self):
        for step in range(self.ring.planes):
            self.across(step).wait_recv()

    def drain(self):
        for step in range(self.ring.planes):
            self.across(step).wait_send()
        for step, flip in self.outs():
            self.plane_out(step, flip).wait_send()
        for step in range(1, self.ring.planes):
            self.plane_back(step).wait_send()
        for step in range(1, self.ring.lines):
            self.line_out(step).wait_send()


def step_kernel(slabs, lines, cuts, factor, *refs):
    chunks = len(cuts)
    starts = [sum(cuts[:at]) for at in range(chunks)]
    sources, refs = refs[:13], refs[13:]
    (first_out, second_out, third_out), refs = refs[:3], refs[3:]
    loaded, load_sems, refs = refs[:13], refs[13], refs[14:]
    (p1, p2, p3, w1b, w2p, w3p, a2, even3, odd3, even2, odd2, rows2, g2), refs = refs[:13], refs[13:]
    outgoing, vol, vol_sems, late_own, early_own, *parts = refs
    ring = Ring(slabs, lines)
    ready = ring.greet()
    load = Load(sources, loaded, load_sems)
    load.start()
    late = [
        Summed(ring, *DIRECT[min(at, 1)], late_own.at[pl.ds(starts[at], cuts[at])], *parts[9 * at : 9 * at + 9])
        for at in range(chunks)
    ]
    early = Summed(ring, *DIRECT[2], early_own, *parts[9 * chunks :])

    raw = load.get(0)
    for part in range(slabs):
        outgoing[part] = jnp.concatenate([raw[part, k] for k in range(raw.shape[1])], axis=1)
    ready()
    incoming = Exchange(outgoing, vol, vol_sems, slabs, ring)
    incoming.start()

    f32 = jnp.float32
    channels = raw.shape[1]
    w1, w2, w3, mg = load.get(1), load.get(2), load.get(3), load.get(4)
    spread, pick1, pick2, pick3, back2, back3, taps, order = [load.get(at) for at in range(5, 13)]
    c1, c2, c3 = w1.shape[0], w2.shape[0], w3.shape[1]
    blocks = spread.shape[1] // 128
    plane1, plane2 = pick1.shape[0] // 9, pick2.shape[0] // 9
    length2 = mg.shape[0] // plane2
    width1 = blocks * BLOCK * c1
    width2 = length2 * c2

    wide = contract(w1[...], taps[...])
    for pair in range(9):
        tile = wide[:, pair * 128 : (pair + 1) * 128]
        for l in range(BLOCK):
            moved = pltpu.roll(tile, 2 * l * channels, 1) if l else tile
            w1b[l * c1 : (l + 1) * c1, pair * 128 : (pair + 1) * 128] = half(moved)
    w2p[...] = jnp.zeros_like(w2p)
    w3p[...] = jnp.zeros_like(w3p)
    for pair in range(9):
        w2p[:, pair * 128 : pair * 128 + 3 * c1] = w2[:, pair * 3 * c1 : (pair + 1) * 3 * c1]
        w3p[pair * 256 : pair * 256 + 3 * c2, :] = w3[pair * 3 * c2 : (pair + 1) * 3 * c2, :]

    given = contract(order[...], mg[...])
    late_own[27 * c2 :, :] = jnp.zeros((late_own.shape[0] - 27 * c2, c3), jnp.bfloat16)
    early_own[...] = jnp.zeros_like(early_own)
    incoming.wait_all()
    levels = [half(contract(vol[part], spread[...])) for part in range(slabs)]
    r1 = half(contract(pick1[...], jnp.concatenate(levels, axis=0)))
    for pair in range(9):
        for block in range(blocks):
            p1[block * plane1 : (block + 1) * plane1, pair * 128 : (pair + 1) * 128] = r1[
                pair * plane1 : (pair + 1) * plane1, block * 128 : (block + 1) * 128
            ]
    pre1 = contract(p1[...], w1b[...], 1)
    act1 = half(pre1 * sigmoid(pre1))
    a1 = jnp.concatenate(
        [act1[block * plane1 : (block + 1) * plane1, :] for block in range(blocks)], axis=1
    )
    r2 = contract(pick2[...], a1)
    r2 = jnp.concatenate([r2, jnp.zeros((9 * plane2, 128), f32)], axis=1)
    sides = (half(pltpu.roll(r2, c1, 1)), half(pltpu.roll(r2, width1 + 128 - c1, 1)))
    for l in range(length2):
        chunk = sides[l % 2][:, (l // 2) * 128 : (l // 2 + 1) * 128]
        for pair in range(9):
            p2[l * plane2 : (l + 1) * plane2, pair * 128 : (pair + 1) * 128] = chunk[
                pair * plane2 : (pair + 1) * plane2, :
            ]
    pre2 = contract(p2[...], w2p[...], 1)
    act2 = pre2 * sigmoid(pre2)
    for l in range(length2):
        a2[:, l * c2 : (l + 1) * c2] = act2[l * plane2 : (l + 1) * plane2, :]
    r3 = contract(pick3[...], half(a2[...]))
    r3 = jnp.concatenate([r3, jnp.zeros((9 * plane2, 256), f32)], axis=1)
    sides = (half(pltpu.roll(r3, c2, 1)), half(r3))
    for l in range(length2):
        chunk = sides[l % 2][:, (l // 2) * 128 : (l // 2) * 128 + 256]
        for pair in range(9):
            p3[l * plane2 : (l + 1) * plane2, pair * 256 : (pair + 1) * 256] = chunk[
                pair * plane2 : (pair + 1) * plane2, :
            ]
    pre3 = contract(p3[...], w3p[...])
    slope3 = given * slope_of(pre3)
    delta3 = half(slope3)
    grad3 = contract(half(slope3.T), p3[...])
    for pair in range(9):
        for lane in range(0, 3 * c2, 128):
            wide = min(128, 3 * c2 - lane)
            turned = grad3[:, pair * 256 + lane : pair * 256 + lane + 128].T
            at = pair * 3 * c2 + lane
            late_own[at : at + wide, :] = half(turned[:wide, :])
    for chunk in late:
        chunk.begin()

    spread3 = contract(delta3, w3p[...], 1)
    for pair in range(9):
        for side, holder in ((0, even3), (1, odd3)):
            for tile in range(length2 // 2 + 1):
                total = None
                for part in range(2):
                    l = 2 * (tile - part) + side
                    if 0 <= l < length2:
                        piece = spread3[
                            l * plane2 : (l + 1) * plane2,
                            pair * 256 + part * 128 : pair * 256 + part * 128 + 128,
                        ]
                        total = piece if total is None else total + piece
                holder[pair * plane2 : (pair + 1) * plane2, tile * 128 : (tile + 1) * 128] = total
    down = contract_fine(back3[...], even3[...])
    down = pltpu.roll(down, down.shape[1] - c2, 1) + contract_fine(back3[...], odd3[...])
    for l in range(length2):
        rows2[l * plane2 : (l + 1) * plane2, :] = down[:, l * c2 : (l + 1) * c2]
    slope2 = half(rows2[...]).astype(f32) * slope_of(pre2)
    delta2 = half(slope2)
    for chunk in late:
        chunk.scatter()
    grad2 = contract(half(slope2.T), p2[...])
    g2[...] = jnp.zeros_like(g2)
    for pair in range(9):
        g2[:, pair * 3 * c1 : (pair + 1) * 3 * c1] = grad2[:, pair * 128 : pair * 128 + 3 * c1]

    spread2 = contract(delta2, w2p[...])
    for pair in range(9):
        for l in range(length2):
            holder = odd2 if l % 2 else even2
            holder[pair * plane2 : (pair + 1) * plane2, (l // 2) * 128 : (l // 2 + 1) * 128] = spread2[
                l * plane2 : (l + 1) * plane2, pair * 128 : (pair + 1) * 128
            ]
    tail = jnp.zeros((plane1, 128), f32)
    left = jnp.concatenate([contract_fine(back2[...], even2[...]), tail], axis=1)
    right = jnp.concatenate([contract_fine(back2[...], odd2[...]), tail], axis=1)
    down = pltpu.roll(left, width1 + 128 - c1, 1) + pltpu.roll(right, c1, 1)
    step = BLOCK * c1
    down = jnp.concatenate([down[:, block * step : (block + 1) * step] for block in range(blocks)], axis=0)
    slope1 = down * slope_of(pre1)
    grad1 = contract(half(slope1.T), p1[...])
    tiles = []
    for pair in range(9):
        total = grad1[:c1, pair * 128 : (pair + 1) * 128]
        for l in range(1, BLOCK):
            tile = grad1[l * c1 : (l + 1) * c1, pair * 128 : (pair + 1) * 128]
            total = total + pltpu.roll(tile, 128 - 2 * l * channels, 1)
        tiles.append(half(total))
    first = contract(jnp.concatenate(tiles, axis=1), taps[...], 1)

    tiles2 = g2.shape[1] // 128
    for tile in range(tiles2):
        early_own[tile * c2 : (tile + 1) * c2, :] = half(g2[:, tile * 128 : (tile + 1) * 128])
    early_own[tiles2 * c2 : tiles2 * c2 + c1, : first.shape[1]] = half(first)
    early.begin()
    late[0].gather_plane()
    early.scatter()
    for chunk in late[1:]:
        chunk.gather_plane()
    early.gather_plane()
    for chunk in late:
        chunk.gather_line()
        chunk.spread()
    early.gather_line()
    early.spread()
    for chunk in late:
        chunk.pass_on()
    for at, chunk in enumerate(late):
        chunk.settle()
        low, high = starts[at], min(27 * c2, starts[at] + cuts[at])
        third_out[low:high, :] = chunk.whole[: high - low, :].astype(f32) * factor
    early.pass_on()
    early.settle()
    for tile in range(tiles2):
        wide = min(128, second_out.shape[1] - tile * 128)
        value = early.whole[tile * c2 : (tile + 1) * c2, :].astype(f32) * factor
        second_out[:, tile * 128 : tile * 128 + wide] = value[:, :wide]
    value = early.whole[tiles2 * c2 : tiles2 * c2 + c1, :].astype(f32) * factor
    first_out[...] = value[:, : first_out.shape[1]]
    for part in (*late, early, incoming):
        part.drain()


def flush_kernel(splits, *refs):
    sources, targets, sems = refs[:3], refs[3:6], refs[6]
    copies = []
    for source, target, split in zip(sources, targets, splits):
        rows = source.shape[0] // split
        for at in range(split):
            part = pl.ds(at * rows, rows)
            copies.append(
                pltpu.make_async_copy(source.at[part], target.at[part], sems.at[len(copies)])
            )
    for copy in copies:
        copy.start()
    for copy in copies:
        copy.wait()


def per_device(volumes, w_first, w_second, w_third, map_grad):
    slabs = lax.axis_size("slab")
    devices = lax.axis_size("vol") * slabs
    chips = devices // 2
    lines = chips // (2 * slabs)
    factor = 1.0 / (map_grad.shape[0] * devices)
    parts, channels, level, height, width = volumes.shape
    depth = level * slabs
    tables = tables_of(channels, depth, height, width)
    c1, c2, c3 = w_first.shape[0], w_second.shape[0], w_third.shape[0]
    plane1 = depth * height // 4
    plane2 = depth * height // 16
    length2 = width // 4
    cells = plane2 * length2
    bf16, f32 = jnp.bfloat16, jnp.float32
    planes = 2 * slabs
    tiles2 = pl.cdiv(27 * c1, 128)
    cuts = cuts_of(27 * c2, planes, SHARES)
    early_rows = chunk_rows(tiles2 * c2 + c1, planes)
    operands = (
        volumes.reshape(parts, channels, level * height, width),
        w_first,
        w_second,
        w_third.T,
        map_grad[0].transpose(1, 2, 3, 0).reshape(cells, c3),
        *tables,
    )
    dma = pltpu.SemaphoreType.DMA
    scratch = [(operand.shape, operand.dtype) for operand in operands]
    scratch.append(dma((len(operands),)))
    scratch += [
        ((width // (2 * BLOCK) * plane1, 9 * 128), bf16),
        ((cells, 9 * 128), bf16),
        ((cells, 9 * 256), bf16),
        ((BLOCK * c1, 9 * 128), bf16),
        ((c2, 9 * 128), bf16),
        ((9 * 256, c3), bf16),
        ((plane2, length2 * c2), f32),
        ((9 * plane2, length2 * c2 + 128), f32),
        ((9 * plane2, length2 * c2 + 128), f32),
        ((9 * plane2, width // 2 * c1), f32),
        ((9 * plane2, width // 2 * c1), f32),
        ((cells, c2), f32),
        ((c2, tiles2 * 128), f32),
        ((slabs, level * height, channels * width), bf16),
        ((slabs, level * height, channels * width), bf16),
        dma((2, slabs)),
        ((sum(cuts), c3), bf16),
        ((early_rows, 128), bf16),
    ]
    for rows in cuts + [early_rows]:
        block = rows // (2 * planes)
        for count in (planes, planes, 2 * planes, 1, lines, 2 * planes):
            scratch.append(((count * block, 128), bf16))
        scratch += [dma((2,)), dma((4, 2, planes)), dma((1, 2, lines))]
    scratch = [pltpu.VMEM(*entry) if isinstance(entry, tuple) else entry for entry in scratch]
    in_hbm = pl.BlockSpec(memory_space=pltpu.HBM)
    in_vmem = pl.BlockSpec(memory_space=pltpu.VMEM)
    results = pl.pallas_call(
        functools.partial(step_kernel, slabs, lines, cuts, factor),
        out_shape=[
            pltpu.VMEM(shape, f32) for shape in (w_first.shape, w_second.shape, (27 * c2, c3))
        ],
        in_specs=[in_hbm] * len(operands),
        out_specs=[in_vmem] * 3,
        scratch_shapes=scratch,
        compiler_params=pltpu.CompilerParams(
            collective_id=0, has_side_effects=True, vmem_limit_bytes=(56) << 20
        ),
        name="step",
    )(*operands)
    splits = SPLITS
    first, second, third = pl.pallas_call(
        functools.partial(flush_kernel, splits),
        out_shape=[jax.ShapeDtypeStruct(result.shape, f32) for result in results],
        in_specs=[in_vmem] * 3,
        out_specs=[in_hbm] * 3,
        scratch_shapes=[dma((sum(splits),))],
        compiler_params=pltpu.CompilerParams(vmem_limit_bytes=4 << 20),
        name="flush",
    )(*results)
    return first, second, third.T


def solution(mesh):
    return jax.shard_map(
        per_device,
        mesh=mesh,
        in_specs=(
            P("vol", None, "slab", None, None),
            P(),
            P(),
            P(),
            P(("vol", "slab"), None, None, None, None),
        ),
        out_specs=(P(), P(), P()),
        check_vma=False,
    )
```

```python
import functools

import jax
import jax.numpy as jnp
import numpy as np
from jax import lax
from jax.experimental import pallas as pl
from jax.experimental.pallas import tpu as pltpu
from jax.sharding import PartitionSpec as P

MESH = pl.DeviceIdType.MESH
BLOCK = 8
SHARES = (7, 7)
DIRECT = ((True, False), (False, False), (True, True))


def one_hot(rows, cols, pairs):
    table = np.zeros((rows, cols), np.float32)
    for row, col in pairs:
        table[row, col] = 1.0
    return table


def cell_picks(depth, height, stride):
    out_depth, out_height = depth // stride, height // stride
    pairs = []
    for a in range(3):
        for b in range(3):
            for i in range(out_depth):
                for j in range(out_height):
                    z, y = stride * i + a - 1, stride * j + b - 1
                    if 0 <= z < depth and 0 <= y < height:
                        row = ((a * 3 + b) * out_depth + i) * out_height + j
                        pairs.append((row, z * height + y))
    return one_hot(9 * out_depth * out_height, depth * height, pairs)


def tables_of(channels, depth, height, width):
    blocks = width // (2 * BLOCK)
    spread = np.zeros((channels, width, blocks * 128), np.float32)
    for block in range(blocks):
        for at in range(2 * BLOCK + 1):
            x = 2 * BLOCK * block - 1 + at
            if x >= 0:
                for k in range(channels):
                    spread[k, x, block * 128 + at * channels + k] = 1.0
    taps = one_hot(
        27 * channels,
        9 * 128,
        [
            (pair * 3 * channels + lane, pair * 128 + lane)
            for pair in range(9)
            for lane in range(3 * channels)
        ],
    )
    plane, length = (depth // 4) * (height // 4), width // 4
    order = one_hot(
        plane * length,
        plane * length,
        [(l * plane + p, p * length + l) for l in range(length) for p in range(plane)],
    )
    second = cell_picks(depth // 2, height // 2, 2)
    third = cell_picks(depth // 4, height // 4, 1)
    spread = spread.reshape(channels * width, -1)
    tables = (spread, cell_picks(depth, height, 2), second, third, second.T, third.T, taps, order)
    return shelve(tables)


def shelve(tables):
    places, shelf, lane, height = {}, 0, 0, 0
    width = max(pl.cdiv(table.shape[1], 128) * 128 for table in tables)
    for at in sorted(range(len(tables)), key=lambda at: (-tables[at].shape[0], at)):
        rows, cols = tables[at].shape
        if lane + cols > width:
            shelf, lane, height = shelf + height, 0, 0
        places[at] = (shelf, lane, rows, cols)
        lane += pl.cdiv(cols, 128) * 128
        height = max(height, pl.cdiv(rows, 16) * 16)
    packed = np.zeros((shelf + height, width), np.float32)
    for at, (row, lane, rows, cols) in places.items():
        packed[row : row + rows, lane : lane + cols] = tables[at]
    return jnp.asarray(packed, jnp.bfloat16), [places[at] for at in range(len(tables))]


def contract(lhs, rhs, rhs_dim=0):
    return lax.dot_general(
        lhs, rhs, (((1,), (rhs_dim,)), ((), ())), preferred_element_type=jnp.float32
    )


def contract_fine(lhs, rhs):
    coarse = half(rhs)
    return contract(lhs, coarse) + contract(lhs, half(rhs - coarse.astype(jnp.float32)))


def sigmoid(pre):
    return 1.0 / (1.0 + jnp.exp(-pre))


def slope_of(pre):
    sigma = sigmoid(pre)
    return sigma * (1.0 + pre * (1.0 - sigma))


def half(value):
    return value.astype(jnp.bfloat16)


def chunk_rows(rows, planes):
    return pl.cdiv(rows, 32 * planes) * 32 * planes


def cuts_of(rows, planes, shares):
    units = chunk_rows(rows, planes) // (32 * planes)
    bounds = [units * sum(shares[:at]) // sum(shares) for at in range(len(shares) + 1)]
    return [32 * planes * (high - low) for low, high in zip(bounds, bounds[1:]) if high > low]


class Load:
    def __init__(self, sources, targets, sems):
        self.copies = [
            pltpu.make_async_copy(source, target, sems.at[index])
            for index, (source, target) in enumerate(zip(sources, targets))
        ]
        self.targets = targets

    def start(self):
        for copy in self.copies:
            copy.start()

    def get(self, index):
        self.copies[index].wait()
        return self.targets[index]


class Exchange:
    def __init__(self, source, held, sems, slabs, ring):
        self.slabs = slabs
        self.source, self.held, self.sems = source, held, sems
        self.vol, self.slab = ring.vol, ring.slab

    def copy(self, source, target, other):
        return pltpu.make_async_remote_copy(
            src_ref=source,
            dst_ref=target,
            send_sem=self.sems.at[0],
            recv_sem=self.sems.at[1],
            device_id=(self.vol, other),
            device_id_type=MESH,
        )

    def start(self):
        for step in range(1, self.slabs):
            other = lax.rem(self.slab + step, self.slabs)
            self.copy(self.source.at[other], self.held.at[self.slab], other).start()
        self.held[self.slab] = self.source[self.slab]

    def everything(self):
        other = lax.rem(self.slab + 1, self.slabs)
        rest = pl.ds(0, self.slabs - 1)
        return self.copy(self.source.at[rest], self.held.at[rest], other)

    def wait_all(self):
        self.everything().wait_recv()

    def drain(self):
        self.everything().wait_send()


class Ring:
    def __init__(self, slabs, lines):
        self.slabs, self.lines, self.planes = slabs, lines, 2 * slabs
        self.vol = lax.axis_index("vol")
        self.slab = lax.axis_index("slab")
        self.core = lax.rem(self.vol, 2)
        self.side = lax.rem(self.vol // 2, 2)
        self.at_line = self.vol // 4
        self.at_plane = self.side * slabs + self.slab
        self.half = self.core_of(self.core, self.side, self.at_line)
        self.pair = (self.vol + 1 - 2 * self.core, self.slab)

    def core_of(self, half, side, line):
        return half

    def at(self, line, plane, half):
        side = plane // self.slabs
        core = self.core_of(half, side, line)
        return ((line * 2 + side) * 2 + core, lax.rem(plane, self.slabs))

    def in_plane(self, step, flip=0):
        other = lax.rem(self.at_plane + step, self.planes)
        half = 1 - self.half if flip else self.half
        return other, self.at(self.at_line, other, half)

    def in_line(self, step):
        other = lax.rem(self.at_line + step, self.lines)
        return other, self.at(other, self.at_plane, self.half)

    def greet(self):
        barrier = pltpu.get_barrier_semaphore()
        partners = [self.pair]
        partners += [self.in_plane(step, 0)[1] for step in range(1, self.planes)]
        partners += [self.in_plane(step, 1)[1] for step in range(1, self.planes)]
        partners += [self.in_line(step)[1] for step in range(1, self.lines)]
        for partner in partners:
            pl.semaphore_signal(barrier, inc=1, device_id=partner, device_id_type=MESH)
        return lambda: pl.semaphore_wait(barrier, len(partners))


class Summed:
    SENT_OUT, SENT_LINE, SENT_BACK, OUT, LINE, ACROSS, SWAP, BACK = range(8)

    @staticmethod
    def sems(direct_out, direct, planes):
        return planes + 6 if not direct else 6 if direct_out else 7

    def __init__(self, ring, direct_out, direct, own, from_pair, mine, landed, middle, lined, whole, sems):
        self.ring, self.direct_out, self.direct = ring, direct_out, direct
        self.own, self.from_pair, self.mine = own, from_pair, mine
        self.landed, self.middle, self.lined = landed, middle, lined
        self.whole, self.sems_at = whole, sems
        self.block = middle.shape[0]
        self.rows = ring.planes * self.block
        self.spot = ring.half * ring.planes + ring.at_plane

    def blocks(self, index, count=1):
        if isinstance(index, int):
            return pl.ds(index * self.block, count * self.block)
        return pl.ds(pl.multiple_of(index * self.block, 16), count * self.block)

    def halves(self, index):
        return pl.ds(pl.multiple_of(index * self.rows, 16), self.rows)

    def remote(self, source, target, sent, received, device):
        return pltpu.make_async_remote_copy(
            src_ref=source,
            dst_ref=target,
            send_sem=self.sems_at.at[sent],
            recv_sem=self.sems_at.at[received],
            device_id=device,
            device_id_type=MESH,
        )

    def await_blocks(self, ref, count, received):
        part = ref.at[self.blocks(0, count)]
        self.remote(part, part, self.SENT_OUT, received, self.ring.pair).wait_recv()

    def await_sent(self, count, sent):
        part = self.landed.at[self.blocks(0, count)]
        self.remote(part, part, sent, self.OUT, self.ring.pair).wait_send()

    def swap(self):
        source = self.own.at[self.halves(1 - self.ring.half)]
        return self.remote(source, self.from_pair, self.SENT_OUT, self.SWAP, self.ring.pair)

    def plane_out(self, step, flip=0):
        other, device = self.ring.in_plane(step, flip)
        slot = flip * self.ring.planes + step - 1
        if self.direct_out:
            half_at = 1 - self.ring.half if flip else self.ring.half
            source = self.own.at[self.blocks(half_at * self.ring.planes + other)]
        else:
            source = self.mine.at[self.blocks(other)]
        return self.remote(source, self.landed.at[self.blocks(slot)], self.SENT_OUT, self.OUT, device)

    def outs(self):
        steps = [(step, 0) for step in range(1, self.ring.planes)]
        if self.direct_out:
            steps += [(step, 1) for step in range(self.ring.planes)]
        return steps

    def line_out(self, step):
        target = self.lined.at[self.blocks(step - 1)]
        device = self.ring.in_line(step)[1]
        return self.remote(self.middle, target, self.SENT_LINE, self.LINE, device)

    def plane_back(self, step):
        block = self.whole.at[self.blocks(self.spot)]
        received = self.ACROSS if self.direct else self.BACK + step - 1
        return self.remote(block, block, self.SENT_BACK, received, self.ring.in_plane(step)[1])

    def across(self, step):
        planes = self.ring.planes
        if self.direct:
            source, device = self.ring.at_plane, self.ring.in_plane(step, 1)[1]
        else:
            source, device = lax.rem(self.ring.at_plane - step + planes, planes), self.ring.pair
        block = self.whole.at[self.blocks(self.ring.half * planes + source)]
        return self.remote(block, block, self.SENT_BACK, self.ACROSS, device)

    def begin(self):
        if self.direct_out:
            for step, flip in self.outs():
                self.plane_out(step, flip).start()
        else:
            self.swap().start()

    def scatter(self):
        if self.direct_out:
            return
        self.swap().wait_recv()
        own = self.own[self.halves(self.ring.half), :].astype(jnp.float32)
        self.mine[...] = half(own + self.from_pair[...].astype(jnp.float32))
        for step, flip in self.outs():
            self.plane_out(step, flip).start()

    def gather_plane(self):
        if self.direct_out:
            running = self.own[self.blocks(self.spot), :].astype(jnp.float32)
        else:
            running = self.mine[self.blocks(self.ring.at_plane), :].astype(jnp.float32)
        count = len(self.outs())
        self.await_blocks(self.landed, count, self.OUT)
        for slot in range(count):
            running = running + self.landed[self.blocks(slot), :].astype(jnp.float32)
        self.middle[...] = half(running)
        self.lined[self.blocks(self.ring.lines - 1), :] = self.middle[...]
        for step in range(1, self.ring.lines):
            self.line_out(step).start()

    def gather_line(self):
        self.await_blocks(self.lined, self.ring.lines - 1, self.LINE)
        line, lines = self.ring.at_line, self.ring.lines
        running = None
        for source in range(lines):
            slot = lax.rem(line - source + lines - 1, lines)
            value = self.lined[self.blocks(slot), :].astype(jnp.float32)
            running = value if running is None else running + value
        self.whole[self.blocks(self.spot), :] = half(running)

    def spread(self):
        for step in range(1, self.ring.planes):
            self.plane_back(step).start()
            if self.direct:
                self.across(step).start()
        self.across(0).start()

    def pass_on(self):
        if self.direct:
            return
        for step in range(1, self.ring.planes):
            self.plane_back(step).wait_recv()
            self.across(step).start()

    def settle(self):
        planes = self.ring.planes
        self.await_blocks(self.landed, 2 * planes - 1 if self.direct else planes, self.ACROSS)

    def drain(self):
        planes = self.ring.planes
        self.await_sent(2 * planes - 1, self.SENT_OUT)
        self.await_sent(2 * planes - 1, self.SENT_BACK)
        part = self.lined.at[self.blocks(0, self.ring.lines - 1)]
        self.remote(part, part, self.SENT_LINE, self.LINE, self.ring.pair).wait_send()


def step_kernel(slabs, lines, cuts, factor, places, *refs):
    chunks = len(cuts)
    starts = [sum(cuts[:at]) for at in range(chunks)]
    sources, refs = refs[:6], refs[6:]
    (first_out, second_out, third_out), refs = refs[:3], refs[3:]
    loaded, load_sems, refs = refs[:6], refs[6], refs[7:]
    (p1, p2, p3, w1b, w2p, w3p, a2, even3, odd3, even2, odd2, rows2, g2), refs = refs[:13], refs[13:]
    outgoing, vol, vol_sems, late_own, early_own, *parts = refs
    ring = Ring(slabs, lines)
    ready = ring.greet()
    load = Load(sources, loaded, load_sems)
    load.start()
    late = [
        Summed(ring, *DIRECT[min(at, 1)], late_own.at[pl.ds(starts[at], cuts[at])], *parts[7 * at : 7 * at + 7])
        for at in range(chunks)
    ]
    early = Summed(ring, *DIRECT[2], early_own, *parts[7 * chunks :])

    raw = load.get(0)
    for part in range(slabs):
        outgoing[part] = jnp.concatenate([raw[part, k] for k in range(raw.shape[1])], axis=1)
    ready()
    incoming = Exchange(outgoing, vol, vol_sems, slabs, ring)
    incoming.start()

    f32 = jnp.float32
    channels = raw.shape[1]
    w1, w2, w3, mg = load.get(1), load.get(2), load.get(3), load.get(4)
    packed = load.get(5)
    spread, pick1, pick2, pick3, back2, back3, taps, order = [
        packed.at[row : row + rows, lane : lane + cols] for row, lane, rows, cols in places
    ]
    c1, c2, c3 = w1.shape[0], w2.shape[0], w3.shape[1]
    blocks = spread.shape[1] // 128
    plane1, plane2 = pick1.shape[0] // 9, pick2.shape[0] // 9
    length2 = mg.shape[0] // plane2
    width1 = blocks * BLOCK * c1
    width2 = length2 * c2

    wide = contract(w1[...], taps[...])
    for pair in range(9):
        tile = wide[:, pair * 128 : (pair + 1) * 128]
        for l in range(BLOCK):
            moved = pltpu.roll(tile, 2 * l * channels, 1) if l else tile
            w1b[l * c1 : (l + 1) * c1, pair * 128 : (pair + 1) * 128] = half(moved)
    w2p[...] = jnp.zeros_like(w2p)
    w3p[...] = jnp.zeros_like(w3p)
    for pair in range(9):
        w2p[:, pair * 128 : pair * 128 + 3 * c1] = w2[:, pair * 3 * c1 : (pair + 1) * 3 * c1]
        w3p[pair * 256 : pair * 256 + 3 * c2, :] = w3[pair * 3 * c2 : (pair + 1) * 3 * c2, :]

    given = contract(order[...], mg[...])
    late_own[27 * c2 :, :] = jnp.zeros((late_own.shape[0] - 27 * c2, c3), jnp.bfloat16)
    early_own[...] = jnp.zeros_like(early_own)
    incoming.wait_all()
    levels = [half(contract(vol[part], spread[...])) for part in range(slabs)]
    r1 = half(contract(pick1[...], jnp.concatenate(levels, axis=0)))
    for pair in range(9):
        for block in range(blocks):
            p1[block * plane1 : (block + 1) * plane1, pair * 128 : (pair + 1) * 128] = r1[
                pair * plane1 : (pair + 1) * plane1, block * 128 : (block + 1) * 128
            ]
    pre1 = contract(p1[...], w1b[...], 1)
    act1 = half(pre1 * sigmoid(pre1))
    a1 = jnp.concatenate(
        [act1[block * plane1 : (block + 1) * plane1, :] for block in range(blocks)], axis=1
    )
    r2 = contract(pick2[...], a1)
    r2 = jnp.concatenate([r2, jnp.zeros((9 * plane2, 128), f32)], axis=1)
    sides = (half(pltpu.roll(r2, c1, 1)), half(pltpu.roll(r2, width1 + 128 - c1, 1)))
    for l in range(length2):
        chunk = sides[l % 2][:, (l // 2) * 128 : (l // 2 + 1) * 128]
        for pair in range(9):
            p2[l * plane2 : (l + 1) * plane2, pair * 128 : (pair + 1) * 128] = chunk[
                pair * plane2 : (pair + 1) * plane2, :
            ]
    pre2 = contract(p2[...], w2p[...], 1)
    act2 = pre2 * sigmoid(pre2)
    for l in range(length2):
        a2[:, l * c2 : (l + 1) * c2] = act2[l * plane2 : (l + 1) * plane2, :]
    r3 = contract(pick3[...], half(a2[...]))
    r3 = jnp.concatenate([r3, jnp.zeros((9 * plane2, 256), f32)], axis=1)
    sides = (half(pltpu.roll(r3, c2, 1)), half(r3))
    for l in range(length2):
        chunk = sides[l % 2][:, (l // 2) * 128 : (l // 2) * 128 + 256]
        for pair in range(9):
            p3[l * plane2 : (l + 1) * plane2, pair * 256 : (pair + 1) * 256] = chunk[
                pair * plane2 : (pair + 1) * plane2, :
            ]
    pre3 = contract(p3[...], w3p[...])
    slope3 = given * slope_of(pre3)
    delta3 = half(slope3)
    grad3 = contract(half(slope3.T), p3[...])
    for pair in range(9):
        for lane in range(0, 3 * c2, 128):
            wide = min(128, 3 * c2 - lane)
            turned = grad3[:, pair * 256 + lane : pair * 256 + lane + 128].T
            at = pair * 3 * c2 + lane
            late_own[at : at + wide, :] = half(turned[:wide, :])
    for chunk in late:
        chunk.begin()

    spread3 = contract(delta3, w3p[...], 1)
    for pair in range(9):
        for side, holder in ((0, even3), (1, odd3)):
            for tile in range(length2 // 2 + 1):
                total = None
                for part in range(2):
                    l = 2 * (tile - part) + side
                    if 0 <= l < length2:
                        piece = spread3[
                            l * plane2 : (l + 1) * plane2,
                            pair * 256 + part * 128 : pair * 256 + part * 128 + 128,
                        ]
                        total = piece if total is None else total + piece
                holder[pair * plane2 : (pair + 1) * plane2, tile * 128 : (tile + 1) * 128] = total
    down = contract_fine(back3[...], even3[...])
    down = pltpu.roll(down, down.shape[1] - c2, 1) + contract_fine(back3[...], odd3[...])
    for l in range(length2):
        rows2[l * plane2 : (l + 1) * plane2, :] = down[:, l * c2 : (l + 1) * c2]
    slope2 = half(rows2[...]).astype(f32) * slope_of(pre2)
    delta2 = half(slope2)
    for chunk in late:
        chunk.scatter()
    grad2 = contract(half(slope2.T), p2[...])
    g2[...] = jnp.zeros_like(g2)
    for pair in range(9):
        g2[:, pair * 3 * c1 : (pair + 1) * 3 * c1] = grad2[:, pair * 128 : pair * 128 + 3 * c1]

    spread2 = contract(delta2, w2p[...])
    for pair in range(9):
        for l in range(length2):
            holder = odd2 if l % 2 else even2
            holder[pair * plane2 : (pair + 1) * plane2, (l // 2) * 128 : (l // 2 + 1) * 128] = spread2[
                l * plane2 : (l + 1) * plane2, pair * 128 : (pair + 1) * 128
            ]
    tail = jnp.zeros((plane1, 128), f32)
    left = jnp.concatenate([contract_fine(back2[...], even2[...]), tail], axis=1)
    right = jnp.concatenate([contract_fine(back2[...], odd2[...]), tail], axis=1)
    down = pltpu.roll(left, width1 + 128 - c1, 1) + pltpu.roll(right, c1, 1)
    step = BLOCK * c1
    down = jnp.concatenate([down[:, block * step : (block + 1) * step] for block in range(blocks)], axis=0)
    slope1 = down * slope_of(pre1)
    grad1 = contract(half(slope1.T), p1[...])
    tiles = []
    for pair in range(9):
        total = grad1[:c1, pair * 128 : (pair + 1) * 128]
        for l in range(1, BLOCK):
            tile = grad1[l * c1 : (l + 1) * c1, pair * 128 : (pair + 1) * 128]
            total = total + pltpu.roll(tile, 128 - 2 * l * channels, 1)
        tiles.append(half(total))
    first = contract(jnp.concatenate(tiles, axis=1), taps[...], 1)

    tiles2 = g2.shape[1] // 128
    for tile in range(tiles2):
        early_own[tile * c2 : (tile + 1) * c2, :] = half(g2[:, tile * 128 : (tile + 1) * 128])
    early_own[tiles2 * c2 : tiles2 * c2 + c1, : first.shape[1]] = half(first)
    early.begin()
    late[0].gather_plane()
    early.scatter()
    for chunk in late[1:]:
        chunk.gather_plane()
    early.gather_plane()
    for chunk in late:
        chunk.gather_line()
        chunk.spread()
    early.gather_line()
    early.spread()
    for chunk in late:
        chunk.pass_on()
    for at, chunk in enumerate(late):
        chunk.settle()
        low, high = starts[at], min(27 * c2, starts[at] + cuts[at])
        third_out[low:high, :] = chunk.whole[: high - low, :].astype(f32) * factor
    early.pass_on()
    early.settle()
    for tile in range(tiles2):
        wide = min(128, second_out.shape[1] - tile * 128)
        value = early.whole[tile * c2 : (tile + 1) * c2, :].astype(f32) * factor
        second_out[:, tile * 128 : tile * 128 + wide] = value[:, :wide]
    value = early.whole[tiles2 * c2 : tiles2 * c2 + c1, :].astype(f32) * factor
    first_out[...] = value[:, : first_out.shape[1]]
    for part in (*late, early, incoming):
        part.drain()


def flush_kernel(*refs):
    copies = [pltpu.make_async_copy(refs[at], refs[3 + at], refs[6].at[at]) for at in range(3)]
    for copy in copies:
        copy.start()
    for copy in copies:
        copy.wait()


def per_device(volumes, w_first, w_second, w_third, map_grad):
    slabs = lax.axis_size("slab")
    devices = lax.axis_size("vol") * slabs
    chips = devices // 2
    lines = chips // (2 * slabs)
    factor = 1.0 / (map_grad.shape[0] * devices)
    parts, channels, level, height, width = volumes.shape
    depth = level * slabs
    tables, places = tables_of(channels, depth, height, width)
    c1, c2, c3 = w_first.shape[0], w_second.shape[0], w_third.shape[0]
    plane1 = depth * height // 4
    plane2 = depth * height // 16
    length2 = width // 4
    cells = plane2 * length2
    bf16, f32 = jnp.bfloat16, jnp.float32
    planes = 2 * slabs
    tiles2 = pl.cdiv(27 * c1, 128)
    cuts = cuts_of(27 * c2, planes, SHARES)
    early_rows = chunk_rows(tiles2 * c2 + c1, planes)
    operands = (
        volumes.reshape(parts, channels, level * height, width),
        w_first,
        w_second,
        w_third.T,
        map_grad[0].transpose(1, 2, 3, 0).reshape(cells, c3),
        tables,
    )
    dma = pltpu.SemaphoreType.DMA
    scratch = [(operand.shape, operand.dtype) for operand in operands]
    scratch.append(dma((len(operands),)))
    scratch += [
        ((width // (2 * BLOCK) * plane1, 9 * 128), bf16),
        ((cells, 9 * 128), bf16),
        ((cells, 9 * 256), bf16),
        ((BLOCK * c1, 9 * 128), bf16),
        ((c2, 9 * 128), bf16),
        ((9 * 256, c3), bf16),
        ((plane2, length2 * c2), f32),
        ((9 * plane2, length2 * c2 + 128), f32),
        ((9 * plane2, length2 * c2 + 128), f32),
        ((9 * plane2, width // 2 * c1), f32),
        ((9 * plane2, width // 2 * c1), f32),
        ((cells, c2), f32),
        ((c2, tiles2 * 128), f32),
        ((slabs, level * height, channels * width), bf16),
        ((slabs, level * height, channels * width), bf16),
        dma((2,)),
        ((sum(cuts), c3), bf16),
        ((early_rows, 128), bf16),
    ]
    kinds = [DIRECT[min(at, 1)] for at in range(len(cuts))] + [DIRECT[2]]
    for rows, kind in zip(cuts + [early_rows], kinds):
        block = rows // (2 * planes)
        for count in (planes, planes, 2 * planes, 1, lines, 2 * planes):
            scratch.append(((count * block, 128), bf16))
        scratch.append(dma((Summed.sems(*kind, planes),)))
    scratch = [pltpu.VMEM(*entry) if isinstance(entry, tuple) else entry for entry in scratch]
    in_hbm = pl.BlockSpec(memory_space=pltpu.HBM)
    in_vmem = pl.BlockSpec(memory_space=pltpu.VMEM)
    results = pl.pallas_call(
        functools.partial(step_kernel, slabs, lines, cuts, factor, places),
        out_shape=[
            pltpu.VMEM(shape, f32) for shape in (w_first.shape, w_second.shape, (27 * c2, c3))
        ],
        in_specs=[in_hbm] * len(operands),
        out_specs=[in_vmem] * 3,
        scratch_shapes=scratch,
        compiler_params=pltpu.CompilerParams(
            collective_id=0, has_side_effects=True, vmem_limit_bytes=(56) << 20
        ),
        name="step",
    )(*operands)
    first, second, third = pl.pallas_call(
        flush_kernel,
        out_shape=[jax.ShapeDtypeStruct(result.shape, f32) for result in results],
        in_specs=[in_vmem] * 3,
        out_specs=[in_hbm] * 3,
        scratch_shapes=[dma((3,))],
        compiler_params=pltpu.CompilerParams(vmem_limit_bytes=4 << 20),
        name="flush",
    )(*results)
    return first, second, third.T


def solution(mesh):
    return jax.shard_map(
        per_device,
        mesh=mesh,
        in_specs=(
            P("vol", None, "slab", None, None),
            P(),
            P(),
            P(),
            P(("vol", "slab"), None, None, None, None),
        ),
        out_specs=(P(), P(), P()),
        check_vma=False,
    )
```

```python
import functools

import jax
import jax.numpy as jnp
import numpy as np
from jax import lax
from jax.experimental import pallas as pl
from jax.experimental.pallas import tpu as pltpu
from jax.sharding import PartitionSpec as P

MESH = pl.DeviceIdType.MESH
BLOCK = 8
SHARES = (7, 7)
DIRECT = ((True, False), (False, False), (False, True))


def one_hot(rows, cols, pairs):
    table = np.zeros((rows, cols), np.float32)
    for row, col in pairs:
        table[row, col] = 1.0
    return table


def cell_picks(depth, height, stride):
    out_depth, out_height = depth // stride, height // stride
    pairs = []
    for a in range(3):
        for b in range(3):
            for i in range(out_depth):
                for j in range(out_height):
                    z, y = stride * i + a - 1, stride * j + b - 1
                    if 0 <= z < depth and 0 <= y < height:
                        row = ((a * 3 + b) * out_depth + i) * out_height + j
                        pairs.append((row, z * height + y))
    return one_hot(9 * out_depth * out_height, depth * height, pairs)


def tables_of(channels, depth, height, width):
    blocks = width // (2 * BLOCK)
    spread = np.zeros((channels, width, blocks * 128), np.float32)
    for block in range(blocks):
        for at in range(2 * BLOCK + 1):
            x = 2 * BLOCK * block - 1 + at
            if x >= 0:
                for k in range(channels):
                    spread[k, x, block * 128 + at * channels + k] = 1.0
    taps = one_hot(
        27 * channels,
        9 * 128,
        [
            (pair * 3 * channels + lane, pair * 128 + lane)
            for pair in range(9)
            for lane in range(3 * channels)
        ],
    )
    plane, length = (depth // 4) * (height // 4), width // 4
    order = one_hot(
        plane * length,
        plane * length,
        [(l * plane + p, p * length + l) for l in range(length) for p in range(plane)],
    )
    second = cell_picks(depth // 2, height // 2, 2)
    third = cell_picks(depth // 4, height // 4, 1)
    spread = spread.reshape(channels * width, -1)
    tables = (spread, cell_picks(depth, height, 2), second, third, second.T, third.T, taps, order)
    return shelve(tables)


def shelve(tables):
    places, shelf, lane, height = {}, 0, 0, 0
    width = max(pl.cdiv(table.shape[1], 128) * 128 for table in tables)
    for at in sorted(range(len(tables)), key=lambda at: (-tables[at].shape[0], at)):
        rows, cols = tables[at].shape
        if lane + cols > width:
            shelf, lane, height = shelf + height, 0, 0
        places[at] = (shelf, lane, rows, cols)
        lane += pl.cdiv(cols, 128) * 128
        height = max(height, pl.cdiv(rows, 16) * 16)
    packed = np.zeros((shelf + height, width), np.float32)
    for at, (row, lane, rows, cols) in places.items():
        packed[row : row + rows, lane : lane + cols] = tables[at]
    return jnp.asarray(packed, jnp.bfloat16), [places[at] for at in range(len(tables))]


def contract(lhs, rhs, rhs_dim=0):
    return lax.dot_general(
        lhs, rhs, (((1,), (rhs_dim,)), ((), ())), preferred_element_type=jnp.float32
    )


def contract_fine(lhs, rhs):
    coarse = half(rhs)
    return contract(lhs, coarse) + contract(lhs, half(rhs - coarse.astype(jnp.float32)))


def sigmoid(pre):
    return 1.0 / (1.0 + jnp.exp(-pre))


def slope_of(pre):
    sigma = sigmoid(pre)
    return sigma * (1.0 + pre * (1.0 - sigma))


def half(value):
    return value.astype(jnp.bfloat16)


def chunk_rows(rows, planes):
    return pl.cdiv(rows, 32 * planes) * 32 * planes


def cuts_of(rows, planes, shares):
    units = chunk_rows(rows, planes) // (32 * planes)
    bounds = [units * sum(shares[:at]) // sum(shares) for at in range(len(shares) + 1)]
    return [32 * planes * (high - low) for low, high in zip(bounds, bounds[1:]) if high > low]


class Load:
    def __init__(self, sources, targets, sems):
        self.copies = [
            pltpu.make_async_copy(source, target, sems.at[index])
            for index, (source, target) in enumerate(zip(sources, targets))
        ]
        self.targets = targets

    def start(self):
        for copy in self.copies:
            copy.start()

    def get(self, index):
        self.copies[index].wait()
        return self.targets[index]


class Exchange:
    def __init__(self, source, held, sems, slabs, ring):
        self.slabs = slabs
        self.source, self.held, self.sems = source, held, sems
        self.vol, self.slab = ring.vol, ring.slab

    def copy(self, source, target, other):
        return pltpu.make_async_remote_copy(
            src_ref=source,
            dst_ref=target,
            send_sem=self.sems.at[0],
            recv_sem=self.sems.at[1],
            device_id=(self.vol, other),
            device_id_type=MESH,
        )

    def start(self):
        for step in range(1, self.slabs):
            other = lax.rem(self.slab + step, self.slabs)
            self.copy(self.source.at[other], self.held.at[self.slab], other).start()
        self.held[self.slab] = self.source[self.slab]

    def everything(self):
        other = lax.rem(self.slab + 1, self.slabs)
        rest = pl.ds(0, self.slabs - 1)
        return self.copy(self.source.at[rest], self.held.at[rest], other)

    def wait_all(self):
        self.everything().wait_recv()

    def drain(self):
        self.everything().wait_send()


class Ring:
    def __init__(self, slabs, lines):
        self.slabs, self.lines, self.planes = slabs, lines, 2 * slabs
        self.vol = lax.axis_index("vol")
        self.slab = lax.axis_index("slab")
        self.core = lax.rem(self.vol, 2)
        self.side = lax.rem(self.vol // 2, 2)
        self.at_line = self.vol // 4
        self.at_plane = self.side * slabs + self.slab
        self.half = self.core_of(self.core, self.side, self.at_line)
        self.pair = (self.vol + 1 - 2 * self.core, self.slab)

    def core_of(self, half, side, line):
        return half

    def at(self, line, plane, half):
        side = plane // self.slabs
        core = self.core_of(half, side, line)
        return ((line * 2 + side) * 2 + core, lax.rem(plane, self.slabs))

    def in_plane(self, step, flip=0):
        other = lax.rem(self.at_plane + step, self.planes)
        half = 1 - self.half if flip else self.half
        return other, self.at(self.at_line, other, half)

    def in_line(self, step):
        other = lax.rem(self.at_line + step, self.lines)
        return other, self.at(other, self.at_plane, self.half)

    def greet(self):
        barrier = pltpu.get_barrier_semaphore()
        partners = [self.pair]
        partners += [self.in_plane(step, 0)[1] for step in range(1, self.planes)]
        partners += [self.in_plane(step, 1)[1] for step in range(1, self.planes)]
        partners += [self.in_line(step)[1] for step in range(1, self.lines)]
        for partner in partners:
            pl.semaphore_signal(barrier, inc=1, device_id=partner, device_id_type=MESH)
        return lambda: pl.semaphore_wait(barrier, len(partners))


class Summed:
    OUT, LINE, ACROSS, SWAP = range(4)

    @staticmethod
    def sems(direct_out, direct, planes):
        return (3 if direct_out else 4) + (0 if direct else planes - 1)

    @staticmethod
    def sent_rows(rows, planes, lines):
        return rows // (2 * planes) * (2 * (2 * planes - 1) + lines - 1)

    def __init__(self, ring, sent, direct_out, direct, own, from_pair, mine, landed, middle, lined, whole, sems):
        self.ring, self.direct_out, self.direct = ring, direct_out, direct
        self.own, self.from_pair, self.mine = own, from_pair, mine
        self.landed, self.middle, self.lined = landed, middle, lined
        self.whole, self.sems_at, self.sent = whole, sems, sent
        self.block = middle.shape[0]
        self.rows = ring.planes * self.block
        self.spot = ring.half * ring.planes + ring.at_plane

    def blocks(self, index, count=1):
        if isinstance(index, int):
            return pl.ds(index * self.block, count * self.block)
        return pl.ds(pl.multiple_of(index * self.block, 16), count * self.block)

    def halves(self, index):
        return pl.ds(pl.multiple_of(index * self.rows, 16), self.rows)

    def remote(self, source, target, received, device):
        return pltpu.make_async_remote_copy(
            src_ref=source,
            dst_ref=target,
            send_sem=self.sent.at[0],
            recv_sem=self.sems_at.at[received],
            device_id=device,
            device_id_type=MESH,
        )

    def await_blocks(self, ref, count, received):
        part = ref.at[self.blocks(0, count)]
        self.remote(part, part, received, self.ring.pair).wait_recv()

    def swap(self):
        source = self.own.at[self.halves(1 - self.ring.half)]
        return self.remote(source, self.from_pair, self.SWAP, self.ring.pair)

    def plane_out(self, step, flip=0):
        other, device = self.ring.in_plane(step, flip)
        slot = flip * self.ring.planes + step - 1
        if self.direct_out:
            half_at = 1 - self.ring.half if flip else self.ring.half
            source = self.own.at[self.blocks(half_at * self.ring.planes + other)]
        else:
            source = self.mine.at[self.blocks(other)]
        return self.remote(source, self.landed.at[self.blocks(slot)], self.OUT, device)

    def outs(self):
        steps = [(step, 0) for step in range(1, self.ring.planes)]
        if self.direct_out:
            steps += [(step, 1) for step in range(self.ring.planes)]
        return steps

    def line_out(self, step):
        target = self.lined.at[self.blocks(step - 1)]
        device = self.ring.in_line(step)[1]
        return self.remote(self.middle, target, self.LINE, device)

    def plane_back(self, step):
        block = self.whole.at[self.blocks(self.spot)]
        received = self.ACROSS if self.direct else (2 if self.direct_out else 3) + step
        return self.remote(block, block, received, self.ring.in_plane(step)[1])

    def across(self, step):
        planes = self.ring.planes
        if self.direct:
            source, device = self.ring.at_plane, self.ring.in_plane(step, 1)[1]
        else:
            source, device = lax.rem(self.ring.at_plane - step + planes, planes), self.ring.pair
        block = self.whole.at[self.blocks(self.ring.half * planes + source)]
        return self.remote(block, block, self.ACROSS, device)

    def begin(self):
        if self.direct_out:
            for step, flip in self.outs():
                self.plane_out(step, flip).start()
        else:
            self.swap().start()

    def scatter(self):
        if self.direct_out:
            return
        self.swap().wait_recv()
        own = self.own[self.halves(self.ring.half), :].astype(jnp.float32)
        self.mine[...] = half(own + self.from_pair[...].astype(jnp.float32))
        for step, flip in self.outs():
            self.plane_out(step, flip).start()

    def gather_plane(self):
        if self.direct_out:
            running = self.own[self.blocks(self.spot), :].astype(jnp.float32)
        else:
            running = self.mine[self.blocks(self.ring.at_plane), :].astype(jnp.float32)
        count = len(self.outs())
        self.await_blocks(self.landed, count, self.OUT)
        for slot in range(count):
            running = running + self.landed[self.blocks(slot), :].astype(jnp.float32)
        self.middle[...] = half(running)
        self.lined[self.blocks(self.ring.lines - 1), :] = self.middle[...]
        for step in range(1, self.ring.lines):
            self.line_out(step).start()

    def gather_line(self):
        self.await_blocks(self.lined, self.ring.lines - 1, self.LINE)
        line, lines = self.ring.at_line, self.ring.lines
        running = None
        for source in range(lines):
            slot = lax.rem(line - source + lines - 1, lines)
            value = self.lined[self.blocks(slot), :].astype(jnp.float32)
            running = value if running is None else running + value
        self.whole[self.blocks(self.spot), :] = half(running)

    def spread(self):
        for step in range(1, self.ring.planes):
            self.plane_back(step).start()
            if self.direct:
                self.across(step).start()
        self.across(0).start()

    def pass_on(self):
        if self.direct:
            return
        for step in range(1, self.ring.planes):
            self.plane_back(step).wait_recv()
            self.across(step).start()

    def settle(self):
        planes = self.ring.planes
        self.await_blocks(self.landed, 2 * planes - 1 if self.direct else planes, self.ACROSS)

    def drain(self, everything):
        self.remote(everything, everything, self.OUT, self.ring.pair).wait_send()


def step_kernel(slabs, lines, cuts, factor, places, *refs):
    chunks = len(cuts)
    starts = [sum(cuts[:at]) for at in range(chunks)]
    sources, refs = refs[:6], refs[6:]
    (first_out, second_out, third_out), refs = refs[:3], refs[3:]
    loaded, load_sems, refs = refs[:6], refs[6], refs[7:]
    (p1, p2, p3, w1b, w2p, w3p, a2, even3, odd3, even2, odd2, rows2, g2), refs = refs[:13], refs[13:]
    outgoing, vol, vol_sems, late_own, early_own, everything, sent, *parts = refs
    ring = Ring(slabs, lines)
    ready = ring.greet()
    load = Load(sources, loaded, load_sems)
    load.start()
    late = [
        Summed(ring, sent, *DIRECT[min(at, 1)], late_own.at[pl.ds(starts[at], cuts[at])], *parts[7 * at : 7 * at + 7])
        for at in range(chunks)
    ]
    early = Summed(ring, sent, *DIRECT[2], early_own, *parts[7 * chunks :])

    raw = load.get(0)
    for part in range(slabs):
        outgoing[part] = jnp.concatenate([raw[part, k] for k in range(raw.shape[1])], axis=1)
    ready()
    incoming = Exchange(outgoing, vol, vol_sems, slabs, ring)
    incoming.start()

    f32 = jnp.float32
    channels = raw.shape[1]
    w1, w2, w3, mg = load.get(1), load.get(2), load.get(3), load.get(4)
    packed = load.get(5)
    spread, pick1, pick2, pick3, back2, back3, taps, order = [
        packed.at[row : row + rows, lane : lane + cols] for row, lane, rows, cols in places
    ]
    c1, c2, c3 = w1.shape[0], w2.shape[0], w3.shape[1]
    blocks = spread.shape[1] // 128
    plane1, plane2 = pick1.shape[0] // 9, pick2.shape[0] // 9
    length2 = mg.shape[0] // plane2
    width1 = blocks * BLOCK * c1
    width2 = length2 * c2

    wide = contract(w1[...], taps[...])
    for pair in range(9):
        tile = wide[:, pair * 128 : (pair + 1) * 128]
        for l in range(BLOCK):
            moved = pltpu.roll(tile, 2 * l * channels, 1) if l else tile
            w1b[l * c1 : (l + 1) * c1, pair * 128 : (pair + 1) * 128] = half(moved)
    w2p[...] = jnp.zeros_like(w2p)
    w3p[...] = jnp.zeros_like(w3p)
    for pair in range(9):
        w2p[:, pair * 128 : pair * 128 + 3 * c1] = w2[:, pair * 3 * c1 : (pair + 1) * 3 * c1]
        w3p[pair * 256 : pair * 256 + 3 * c2, :] = w3[pair * 3 * c2 : (pair + 1) * 3 * c2, :]

    given = contract(order[...], mg[...])
    late_own[27 * c2 :, :] = jnp.zeros((late_own.shape[0] - 27 * c2, c3), jnp.bfloat16)
    early_own[...] = jnp.zeros_like(early_own)
    incoming.wait_all()
    levels = [half(contract(vol[part], spread[...])) for part in range(slabs)]
    r1 = half(contract(pick1[...], jnp.concatenate(levels, axis=0)))
    for pair in range(9):
        for block in range(blocks):
            p1[block * plane1 : (block + 1) * plane1, pair * 128 : (pair + 1) * 128] = r1[
                pair * plane1 : (pair + 1) * plane1, block * 128 : (block + 1) * 128
            ]
    pre1 = contract(p1[...], w1b[...], 1)
    act1 = half(pre1 * sigmoid(pre1))
    a1 = jnp.concatenate(
        [act1[block * plane1 : (block + 1) * plane1, :] for block in range(blocks)], axis=1
    )
    r2 = contract(pick2[...], a1)
    r2 = jnp.concatenate([r2, jnp.zeros((9 * plane2, 128), f32)], axis=1)
    sides = (half(pltpu.roll(r2, c1, 1)), half(pltpu.roll(r2, width1 + 128 - c1, 1)))
    for l in range(length2):
        chunk = sides[l % 2][:, (l // 2) * 128 : (l // 2 + 1) * 128]
        for pair in range(9):
            p2[l * plane2 : (l + 1) * plane2, pair * 128 : (pair + 1) * 128] = chunk[
                pair * plane2 : (pair + 1) * plane2, :
            ]
    pre2 = contract(p2[...], w2p[...], 1)
    act2 = pre2 * sigmoid(pre2)
    for l in range(length2):
        a2[:, l * c2 : (l + 1) * c2] = act2[l * plane2 : (l + 1) * plane2, :]
    r3 = contract(pick3[...], half(a2[...]))
    r3 = jnp.concatenate([r3, jnp.zeros((9 * plane2, 256), f32)], axis=1)
    sides = (half(pltpu.roll(r3, c2, 1)), half(r3))
    for l in range(length2):
        chunk = sides[l % 2][:, (l // 2) * 128 : (l // 2) * 128 + 256]
        for pair in range(9):
            p3[l * plane2 : (l + 1) * plane2, pair * 256 : (pair + 1) * 256] = chunk[
                pair * plane2 : (pair + 1) * plane2, :
            ]
    pre3 = contract(p3[...], w3p[...])
    slope3 = given * slope_of(pre3)
    delta3 = half(slope3)
    grad3 = contract(delta3.T, p3[...])
    for pair in range(9):
        for lane in range(0, 3 * c2, 128):
            wide = min(128, 3 * c2 - lane)
            turned = half(grad3[:, pair * 256 + lane : pair * 256 + lane + 128]).T
            at = pair * 3 * c2 + lane
            begun = [chunk for chunk in range(chunks - 1) if at < starts[chunk] + cuts[chunk] <= at + wide]
            late_own[at : at + wide, :] = turned[:wide, :]
            for chunk in begun:
                late[chunk].begin()
    late[-1].begin()

    spread3 = contract(delta3, w3p[...], 1)
    for pair in range(9):
        for side, holder in ((0, even3), (1, odd3)):
            for tile in range(length2 // 2 + 1):
                total = None
                for part in range(2):
                    l = 2 * (tile - part) + side
                    if 0 <= l < length2:
                        piece = spread3[
                            l * plane2 : (l + 1) * plane2,
                            pair * 256 + part * 128 : pair * 256 + part * 128 + 128,
                        ]
                        total = piece if total is None else total + piece
                holder[pair * plane2 : (pair + 1) * plane2, tile * 128 : (tile + 1) * 128] = total
    down = contract_fine(back3[...], even3[...])
    down = pltpu.roll(down, down.shape[1] - c2, 1) + contract_fine(back3[...], odd3[...])
    for l in range(length2):
        rows2[l * plane2 : (l + 1) * plane2, :] = down[:, l * c2 : (l + 1) * c2]
    slope2 = half(rows2[...]).astype(f32) * slope_of(pre2)
    delta2 = half(slope2)
    for chunk in late:
        chunk.scatter()
    grad2 = contract(half(slope2.T), p2[...])
    g2[...] = jnp.zeros_like(g2)
    for pair in range(9):
        g2[:, pair * 3 * c1 : (pair + 1) * 3 * c1] = grad2[:, pair * 128 : pair * 128 + 3 * c1]

    spread2 = contract(delta2, w2p[...])
    for pair in range(9):
        for l in range(length2):
            holder = odd2 if l % 2 else even2
            holder[pair * plane2 : (pair + 1) * plane2, (l // 2) * 128 : (l // 2 + 1) * 128] = spread2[
                l * plane2 : (l + 1) * plane2, pair * 128 : (pair + 1) * 128
            ]
    tail = jnp.zeros((plane1, 128), f32)
    left = jnp.concatenate([contract_fine(back2[...], even2[...]), tail], axis=1)
    right = jnp.concatenate([contract_fine(back2[...], odd2[...]), tail], axis=1)
    down = pltpu.roll(left, width1 + 128 - c1, 1) + pltpu.roll(right, c1, 1)
    step = BLOCK * c1
    down = jnp.concatenate([down[:, block * step : (block + 1) * step] for block in range(blocks)], axis=0)
    slope1 = down * slope_of(pre1)
    grad1 = contract(half(slope1.T), p1[...])
    tiles = []
    for pair in range(9):
        total = grad1[:c1, pair * 128 : (pair + 1) * 128]
        for l in range(1, BLOCK):
            tile = grad1[l * c1 : (l + 1) * c1, pair * 128 : (pair + 1) * 128]
            total = total + pltpu.roll(tile, 128 - 2 * l * channels, 1)
        tiles.append(half(total))
    first = contract(jnp.concatenate(tiles, axis=1), taps[...], 1)

    tiles2 = g2.shape[1] // 128
    for tile in range(tiles2):
        early_own[tile * c2 : (tile + 1) * c2, :] = half(g2[:, tile * 128 : (tile + 1) * 128])
    early_own[tiles2 * c2 : tiles2 * c2 + c1, : first.shape[1]] = half(first)
    early.begin()
    late[0].gather_plane()
    early.scatter()
    for chunk in late[1:]:
        chunk.gather_plane()
    early.gather_plane()
    for chunk in late:
        chunk.gather_line()
        chunk.spread()
    early.gather_line()
    early.spread()
    for chunk in late:
        chunk.pass_on()
    def finish(at, chunk):
        chunk.settle()
        low, high = starts[at], min(27 * c2, starts[at] + cuts[at])
        third_out[low:high, :] = chunk.whole[: high - low, :].astype(f32) * factor
    for at, chunk in enumerate(late[:-1]):
        finish(at, chunk)
    early.pass_on()
    early.settle()
    for tile in range(tiles2):
        wide = min(128, second_out.shape[1] - tile * 128)
        value = early.whole[tile * c2 : (tile + 1) * c2, :].astype(f32) * factor
        second_out[:, tile * 128 : tile * 128 + wide] = value[:, :wide]
    value = early.whole[tiles2 * c2 : tiles2 * c2 + c1, :].astype(f32) * factor
    first_out[...] = value[:, : first_out.shape[1]]
    finish(chunks - 1, late[-1])
    early.drain(everything)
    incoming.drain()


def flush_kernel(*refs):
    copies = [pltpu.make_async_copy(refs[at], refs[3 + at], refs[6].at[at]) for at in range(3)]
    for copy in copies:
        copy.start()
    for copy in copies:
        copy.wait()


def per_device(volumes, w_first, w_second, w_third, map_grad):
    slabs = lax.axis_size("slab")
    devices = lax.axis_size("vol") * slabs
    chips = devices // 2
    lines = chips // (2 * slabs)
    factor = 1.0 / (map_grad.shape[0] * devices)
    parts, channels, level, height, width = volumes.shape
    depth = level * slabs
    tables, places = tables_of(channels, depth, height, width)
    c1, c2, c3 = w_first.shape[0], w_second.shape[0], w_third.shape[0]
    plane1 = depth * height // 4
    plane2 = depth * height // 16
    length2 = width // 4
    cells = plane2 * length2
    bf16, f32 = jnp.bfloat16, jnp.float32
    planes = 2 * slabs
    tiles2 = pl.cdiv(27 * c1, 128)
    cuts = cuts_of(27 * c2, planes, SHARES)
    early_rows = chunk_rows(tiles2 * c2 + c1, planes)
    operands = (
        volumes.reshape(parts, channels, level * height, width),
        w_first,
        w_second,
        w_third.T,
        map_grad[0].transpose(1, 2, 3, 0).reshape(cells, c3),
        tables,
    )
    dma = pltpu.SemaphoreType.DMA
    scratch = [(operand.shape, operand.dtype) for operand in operands]
    scratch.append(dma((len(operands),)))
    scratch += [
        ((width // (2 * BLOCK) * plane1, 9 * 128), bf16),
        ((cells, 9 * 128), bf16),
        ((cells, 9 * 256), bf16),
        ((BLOCK * c1, 9 * 128), bf16),
        ((c2, 9 * 128), bf16),
        ((9 * 256, c3), bf16),
        ((plane2, length2 * c2), f32),
        ((9 * plane2, length2 * c2 + 128), f32),
        ((9 * plane2, length2 * c2 + 128), f32),
        ((9 * plane2, width // 2 * c1), f32),
        ((9 * plane2, width // 2 * c1), f32),
        ((cells, c2), f32),
        ((c2, tiles2 * 128), f32),
        ((slabs, level * height, channels * width), bf16),
        ((slabs, level * height, channels * width), bf16),
        dma((2,)),
        ((sum(cuts), c3), bf16),
        ((early_rows, 128), bf16),
        ((sum(Summed.sent_rows(rows, planes, lines) for rows in cuts + [early_rows]), 128), bf16),
        dma((1,)),
    ]
    kinds = [DIRECT[min(at, 1)] for at in range(len(cuts))] + [DIRECT[2]]
    for rows, kind in zip(cuts + [early_rows], kinds):
        block = rows // (2 * planes)
        for count in (planes, planes, 2 * planes, 1, lines, 2 * planes):
            scratch.append(((count * block, 128), bf16))
        scratch.append(dma((Summed.sems(*kind, planes),)))
    scratch = [pltpu.VMEM(*entry) if isinstance(entry, tuple) else entry for entry in scratch]
    in_hbm = pl.BlockSpec(memory_space=pltpu.HBM)
    in_vmem = pl.BlockSpec(memory_space=pltpu.VMEM)
    results = pl.pallas_call(
        functools.partial(step_kernel, slabs, lines, cuts, factor, places),
        out_shape=[
            pltpu.VMEM(shape, f32) for shape in (w_first.shape, w_second.shape, (27 * c2, c3))
        ],
        in_specs=[in_hbm] * len(operands),
        out_specs=[in_vmem] * 3,
        scratch_shapes=scratch,
        compiler_params=pltpu.CompilerParams(
            collective_id=0, has_side_effects=True, vmem_limit_bytes=(56) << 20
        ),
        name="step",
    )(*operands)
    first, second, third = pl.pallas_call(
        flush_kernel,
        out_shape=[jax.ShapeDtypeStruct(result.shape, f32) for result in results],
        in_specs=[in_vmem] * 3,
        out_specs=[in_hbm] * 3,
        scratch_shapes=[dma((3,))],
        compiler_params=pltpu.CompilerParams(vmem_limit_bytes=4 << 20),
        name="flush",
    )(*results)
    return first, second, third.T


def solution(mesh):
    return jax.shard_map(
        per_device,
        mesh=mesh,
        in_specs=(
            P("vol", None, "slab", None, None),
            P(),
            P(),
            P(),
            P(("vol", "slab"), None, None, None, None),
        ),
        out_specs=(P(), P(), P()),
        check_vma=False,
    )
```

```python
import functools

import jax
import jax.numpy as jnp
import numpy as np
from jax import lax
from jax.experimental import pallas as pl
from jax.experimental.pallas import tpu as pltpu
from jax.sharding import PartitionSpec as P

MESH = pl.DeviceIdType.MESH
BLOCK = 8
SHARES = (3, 5, 6)
DIRECT = ((True, False), (False, False), (False, True))


def one_hot(rows, cols, pairs):
    table = np.zeros((rows, cols), np.float32)
    for row, col in pairs:
        table[row, col] = 1.0
    return table


def cell_picks(depth, height, stride):
    out_depth, out_height = depth // stride, height // stride
    pairs = []
    for a in range(3):
        for b in range(3):
            for i in range(out_depth):
                for j in range(out_height):
                    z, y = stride * i + a - 1, stride * j + b - 1
                    if 0 <= z < depth and 0 <= y < height:
                        row = ((a * 3 + b) * out_depth + i) * out_height + j
                        pairs.append((row, z * height + y))
    return one_hot(9 * out_depth * out_height, depth * height, pairs)


def tables_of(channels, depth, height, width):
    blocks = width // (2 * BLOCK)
    spread = np.zeros((channels, width, blocks * 128), np.float32)
    for block in range(blocks):
        for at in range(2 * BLOCK + 1):
            x = 2 * BLOCK * block - 1 + at
            if x >= 0:
                for k in range(channels):
                    spread[k, x, block * 128 + at * channels + k] = 1.0
    taps = one_hot(
        27 * channels,
        9 * 128,
        [
            (pair * 3 * channels + lane, pair * 128 + lane)
            for pair in range(9)
            for lane in range(3 * channels)
        ],
    )
    plane, length = (depth // 4) * (height // 4), width // 4
    order = one_hot(
        plane * length,
        plane * length,
        [(l * plane + p, p * length + l) for l in range(length) for p in range(plane)],
    )
    second = cell_picks(depth // 2, height // 2, 2)
    third = cell_picks(depth // 4, height // 4, 1)
    spread = spread.reshape(channels * width, -1)
    tables = (spread, cell_picks(depth, height, 2), second, third, second.T, third.T, taps, order)
    return shelve(tables)


def shelve(tables):
    places, shelf, lane, height = {}, 0, 0, 0
    width = max(pl.cdiv(table.shape[1], 128) * 128 for table in tables)
    for at in sorted(range(len(tables)), key=lambda at: (-tables[at].shape[0], at)):
        rows, cols = tables[at].shape
        if lane + cols > width:
            shelf, lane, height = shelf + height, 0, 0
        places[at] = (shelf, lane, rows, cols)
        lane += pl.cdiv(cols, 128) * 128
        height = max(height, pl.cdiv(rows, 16) * 16)
    packed = np.zeros((shelf + height, width), np.float32)
    for at, (row, lane, rows, cols) in places.items():
        packed[row : row + rows, lane : lane + cols] = tables[at]
    return jnp.asarray(packed, jnp.bfloat16), [places[at] for at in range(len(tables))]


def contract(lhs, rhs, rhs_dim=0):
    return lax.dot_general(
        lhs, rhs, (((1,), (rhs_dim,)), ((), ())), preferred_element_type=jnp.float32
    )


def contract_fine(lhs, rhs):
    coarse = half(rhs)
    return contract(lhs, coarse) + contract(lhs, half(rhs - coarse.astype(jnp.float32)))


def sigmoid(pre):
    return 1.0 / (1.0 + jnp.exp(-pre))


def slope_of(pre):
    sigma = sigmoid(pre)
    return sigma * (1.0 + pre * (1.0 - sigma))


def half(value):
    return value.astype(jnp.bfloat16)


def chunk_rows(rows, planes):
    return pl.cdiv(rows, 32 * planes) * 32 * planes


def cuts_of(rows, planes, shares):
    units = chunk_rows(rows, planes) // (32 * planes)
    bounds = [units * sum(shares[:at]) // sum(shares) for at in range(len(shares) + 1)]
    return [32 * planes * (high - low) for low, high in zip(bounds, bounds[1:]) if high > low]


class Load:
    def __init__(self, sources, targets, sems):
        self.copies = [
            pltpu.make_async_copy(source, target, sems.at[index])
            for index, (source, target) in enumerate(zip(sources, targets))
        ]
        self.targets = targets

    def start(self):
        for copy in self.copies:
            copy.start()

    def get(self, index):
        self.copies[index].wait()
        return self.targets[index]


class Exchange:
    def __init__(self, source, held, sems, slabs, ring):
        self.slabs = slabs
        self.source, self.held, self.sems = source, held, sems
        self.vol, self.slab = ring.vol, ring.slab

    def copy(self, source, target, other):
        return pltpu.make_async_remote_copy(
            src_ref=source,
            dst_ref=target,
            send_sem=self.sems.at[0],
            recv_sem=self.sems.at[1],
            device_id=(self.vol, other),
            device_id_type=MESH,
        )

    def start(self):
        for step in range(1, self.slabs):
            other = lax.rem(self.slab + step, self.slabs)
            self.copy(self.source.at[other], self.held.at[self.slab], other).start()
        self.held[self.slab] = self.source[self.slab]

    def everything(self):
        other = lax.rem(self.slab + 1, self.slabs)
        rest = pl.ds(0, self.slabs - 1)
        return self.copy(self.source.at[rest], self.held.at[rest], other)

    def wait_all(self):
        self.everything().wait_recv()

    def drain(self):
        self.everything().wait_send()


class Ring:
    def __init__(self, slabs, lines):
        self.slabs, self.lines, self.planes = slabs, lines, 2 * slabs
        self.vol = lax.axis_index("vol")
        self.slab = lax.axis_index("slab")
        self.core = lax.rem(self.vol, 2)
        self.side = lax.rem(self.vol // 2, 2)
        self.at_line = self.vol // 4
        self.at_plane = self.side * slabs + self.slab
        self.half = self.core_of(self.core, self.side, self.at_line)
        self.pair = (self.vol + 1 - 2 * self.core, self.slab)

    def core_of(self, half, side, line):
        return half

    def at(self, line, plane, half):
        side = plane // self.slabs
        core = self.core_of(half, side, line)
        return ((line * 2 + side) * 2 + core, lax.rem(plane, self.slabs))

    def in_plane(self, step, flip=0):
        other = lax.rem(self.at_plane + step, self.planes)
        half = 1 - self.half if flip else self.half
        return other, self.at(self.at_line, other, half)

    def in_line(self, step):
        other = lax.rem(self.at_line + step, self.lines)
        return other, self.at(other, self.at_plane, self.half)

    def greet(self):
        barrier = pltpu.get_barrier_semaphore()
        partners = [self.in_plane(step, 0)[1] for step in range(1, self.planes)]
        partners += [self.pair]
        partners += [self.in_plane(step, 1)[1] for step in range(1, self.planes)]
        partners += [self.in_line(step)[1] for step in range(1, self.lines)]
        for partner in partners:
            pl.semaphore_signal(barrier, inc=1, device_id=partner, device_id_type=MESH)
        return lambda: pl.semaphore_wait(barrier, len(partners))


class Summed:
    OUT, LINE, ACROSS, SWAP = range(4)

    @staticmethod
    def sems(direct_out, direct, planes):
        return (3 if direct_out else 4) + (0 if direct else planes - 1)

    @staticmethod
    def sent_rows(rows, planes, lines):
        return rows // (2 * planes) * (2 * (2 * planes - 1) + lines - 1)

    def __init__(self, ring, sent, direct_out, direct, own, from_pair, mine, landed, middle, lined, whole, sems):
        self.ring, self.direct_out, self.direct = ring, direct_out, direct
        self.own, self.from_pair, self.mine = own, from_pair, mine
        self.landed, self.middle, self.lined = landed, middle, lined
        self.whole, self.sems_at, self.sent = whole, sems, sent
        self.block = middle.shape[0]
        self.rows = ring.planes * self.block
        self.spot = ring.half * ring.planes + ring.at_plane

    def blocks(self, index, count=1):
        if isinstance(index, int):
            return pl.ds(index * self.block, count * self.block)
        return pl.ds(pl.multiple_of(index * self.block, 16), count * self.block)

    def halves(self, index):
        return pl.ds(pl.multiple_of(index * self.rows, 16), self.rows)

    def remote(self, source, target, received, device):
        return pltpu.make_async_remote_copy(
            src_ref=source,
            dst_ref=target,
            send_sem=self.sent.at[0],
            recv_sem=self.sems_at.at[received],
            device_id=device,
            device_id_type=MESH,
        )

    def await_blocks(self, ref, count, received):
        part = ref.at[self.blocks(0, count)]
        self.remote(part, part, received, self.ring.pair).wait_recv()

    def swap(self):
        source = self.own.at[self.halves(1 - self.ring.half)]
        return self.remote(source, self.from_pair, self.SWAP, self.ring.pair)

    def plane_out(self, step, flip=0):
        other, device = self.ring.in_plane(step, flip)
        slot = flip * self.ring.planes + step - 1
        if self.direct_out:
            half_at = 1 - self.ring.half if flip else self.ring.half
            source = self.own.at[self.blocks(half_at * self.ring.planes + other)]
        else:
            source = self.mine.at[self.blocks(other)]
        return self.remote(source, self.landed.at[self.blocks(slot)], self.OUT, device)

    def outs(self):
        steps = [(step, 0) for step in range(1, self.ring.planes)]
        if self.direct_out:
            steps += [(step, 1) for step in range(self.ring.planes)]
        return steps

    def line_out(self, step):
        target = self.lined.at[self.blocks(step - 1)]
        device = self.ring.in_line(step)[1]
        return self.remote(self.middle, target, self.LINE, device)

    def plane_back(self, step):
        block = self.whole.at[self.blocks(self.spot)]
        received = self.ACROSS if self.direct else (2 if self.direct_out else 3) + step
        return self.remote(block, block, received, self.ring.in_plane(step)[1])

    def across(self, step):
        planes = self.ring.planes
        if self.direct:
            source, device = self.ring.at_plane, self.ring.in_plane(step, 1)[1]
        else:
            source, device = lax.rem(self.ring.at_plane - step + planes, planes), self.ring.pair
        block = self.whole.at[self.blocks(self.ring.half * planes + source)]
        return self.remote(block, block, self.ACROSS, device)

    def begin(self):
        if self.direct_out:
            for step, flip in self.outs():
                self.plane_out(step, flip).start()
        else:
            self.swap().start()

    def scatter(self):
        if self.direct_out:
            return
        self.swap().wait_recv()
        own = self.own[self.halves(self.ring.half), :].astype(jnp.float32)
        self.mine[...] = half(own + self.from_pair[...].astype(jnp.float32))
        for step, flip in self.outs():
            self.plane_out(step, flip).start()

    def gather_plane(self):
        if self.direct_out:
            running = self.own[self.blocks(self.spot), :].astype(jnp.float32)
        else:
            running = self.mine[self.blocks(self.ring.at_plane), :].astype(jnp.float32)
        count = len(self.outs())
        self.await_blocks(self.landed, count, self.OUT)
        for slot in range(count):
            running = running + self.landed[self.blocks(slot), :].astype(jnp.float32)
        self.middle[...] = half(running)
        self.lined[self.blocks(self.ring.lines - 1), :] = self.middle[...]
        for step in range(1, self.ring.lines):
            self.line_out(step).start()

    def gather_line(self):
        self.await_blocks(self.lined, self.ring.lines - 1, self.LINE)
        line, lines = self.ring.at_line, self.ring.lines
        running = None
        for source in range(lines):
            slot = lax.rem(line - source + lines - 1, lines)
            value = self.lined[self.blocks(slot), :].astype(jnp.float32)
            running = value if running is None else running + value
        self.whole[self.blocks(self.spot), :] = half(running)

    def spread(self):
        for step in range(1, self.ring.planes):
            self.plane_back(step).start()
            if self.direct:
                self.across(step).start()
        self.across(0).start()

    def pass_on(self):
        if self.direct:
            return
        for step in range(1, self.ring.planes):
            self.plane_back(step).wait_recv()
            self.across(step).start()

    def settle(self):
        planes = self.ring.planes
        self.await_blocks(self.landed, 2 * planes - 1 if self.direct else planes, self.ACROSS)

    def drain(self, everything):
        self.remote(everything, everything, self.OUT, self.ring.pair).wait_send()


def step_kernel(slabs, lines, cuts, factor, places, *refs):
    chunks = len(cuts)
    starts = [sum(cuts[:at]) for at in range(chunks)]
    sources, refs = refs[:6], refs[6:]
    (first_out, second_out, third_out), refs = refs[:3], refs[3:]
    loaded, load_sems, refs = refs[:6], refs[6], refs[7:]
    (p1, p2, p3, w1b, w2p, w3p, a2, even3, odd3, even2, odd2, rows2, g2), refs = refs[:13], refs[13:]
    outgoing, vol, vol_sems, late_own, early_own, everything, sent, *parts = refs
    ring = Ring(slabs, lines)
    load = Load(sources, loaded, load_sems)
    load.copies[0].start()
    ready = ring.greet()
    for copy in load.copies[1:]:
        copy.start()
    late = [
        Summed(ring, sent, *DIRECT[min(at, 1)], late_own.at[pl.ds(starts[at], cuts[at])], *parts[7 * at : 7 * at + 7])
        for at in range(chunks)
    ]
    early = Summed(ring, sent, *DIRECT[2], early_own, *parts[7 * chunks :])

    raw = load.get(0)
    for part in range(slabs):
        outgoing[part] = jnp.concatenate([raw[part, k] for k in range(raw.shape[1])], axis=1)
    ready()
    incoming = Exchange(outgoing, vol, vol_sems, slabs, ring)
    incoming.start()

    f32 = jnp.float32
    channels = raw.shape[1]
    w1, w2, w3, mg = load.get(1), load.get(2), load.get(3), load.get(4)
    packed = load.get(5)
    spread, pick1, pick2, pick3, back2, back3, taps, order = [
        packed.at[row : row + rows, lane : lane + cols] for row, lane, rows, cols in places
    ]
    c1, c2, c3 = w1.shape[0], w2.shape[0], w3.shape[1]
    blocks = spread.shape[1] // 128
    plane1, plane2 = pick1.shape[0] // 9, pick2.shape[0] // 9
    length2 = mg.shape[0] // plane2
    width1 = blocks * BLOCK * c1
    width2 = length2 * c2

    wide = contract(w1[...], taps[...])
    for pair in range(9):
        tile = wide[:, pair * 128 : (pair + 1) * 128]
        for l in range(BLOCK):
            moved = pltpu.roll(tile, 2 * l * channels, 1) if l else tile
            w1b[l * c1 : (l + 1) * c1, pair * 128 : (pair + 1) * 128] = half(moved)
    w2p[...] = jnp.zeros_like(w2p)
    w3p[...] = jnp.zeros_like(w3p)
    for pair in range(9):
        w2p[:, pair * 128 : pair * 128 + 3 * c1] = w2[:, pair * 3 * c1 : (pair + 1) * 3 * c1]
        w3p[pair * 256 : pair * 256 + 3 * c2, :] = w3[pair * 3 * c2 : (pair + 1) * 3 * c2, :]

    given = contract(order[...], mg[...])
    late_own[27 * c2 :, :] = jnp.zeros((late_own.shape[0] - 27 * c2, c3), jnp.bfloat16)
    early_own[...] = jnp.zeros_like(early_own)
    incoming.wait_all()
    levels = [half(contract(vol[part], spread[...])) for part in range(slabs)]
    r1 = half(contract(pick1[...], jnp.concatenate(levels, axis=0)))
    for pair in range(9):
        for block in range(blocks):
            p1[block * plane1 : (block + 1) * plane1, pair * 128 : (pair + 1) * 128] = r1[
                pair * plane1 : (pair + 1) * plane1, block * 128 : (block + 1) * 128
            ]
    pre1 = contract(p1[...], w1b[...], 1)
    act1 = half(pre1 * sigmoid(pre1))
    a1 = jnp.concatenate(
        [act1[block * plane1 : (block + 1) * plane1, :] for block in range(blocks)], axis=1
    )
    r2 = contract(pick2[...], a1)
    r2 = jnp.concatenate([r2, jnp.zeros((9 * plane2, 128), f32)], axis=1)
    sides = (half(pltpu.roll(r2, c1, 1)), half(pltpu.roll(r2, width1 + 128 - c1, 1)))
    for l in range(length2):
        chunk = sides[l % 2][:, (l // 2) * 128 : (l // 2 + 1) * 128]
        for pair in range(9):
            p2[l * plane2 : (l + 1) * plane2, pair * 128 : (pair + 1) * 128] = chunk[
                pair * plane2 : (pair + 1) * plane2, :
            ]
    pre2 = contract(p2[...], w2p[...], 1)
    act2 = pre2 * sigmoid(pre2)
    for l in range(length2):
        a2[:, l * c2 : (l + 1) * c2] = act2[l * plane2 : (l + 1) * plane2, :]
    r3 = contract(pick3[...], half(a2[...]))
    r3 = jnp.concatenate([r3, jnp.zeros((9 * plane2, 256), f32)], axis=1)
    sides = (half(pltpu.roll(r3, c2, 1)), half(r3))
    for l in range(length2):
        chunk = sides[l % 2][:, (l // 2) * 128 : (l // 2) * 128 + 256]
        for pair in range(9):
            p3[l * plane2 : (l + 1) * plane2, pair * 256 : (pair + 1) * 256] = chunk[
                pair * plane2 : (pair + 1) * plane2, :
            ]
    pre3 = contract(p3[...], w3p[...])
    slope3 = given * slope_of(pre3)
    delta3 = half(slope3)
    grad3 = contract(delta3.T, p3[...])
    for pair in range(9):
        for lane in range(0, 3 * c2, 128):
            wide = min(128, 3 * c2 - lane)
            turned = half(grad3[:, pair * 256 + lane : pair * 256 + lane + 128]).T
            at = pair * 3 * c2 + lane
            begun = [chunk for chunk in range(chunks - 1) if at < starts[chunk] + cuts[chunk] <= at + wide]
            late_own[at : at + wide, :] = turned[:wide, :]
            for chunk in begun:
                late[chunk].begin()
    late[-1].begin()

    spread3 = contract(delta3, w3p[...], 1)
    for pair in range(9):
        for side, holder in ((0, even3), (1, odd3)):
            for tile in range(length2 // 2 + 1):
                total = None
                for part in range(2):
                    l = 2 * (tile - part) + side
                    if 0 <= l < length2:
                        piece = spread3[
                            l * plane2 : (l + 1) * plane2,
                            pair * 256 + part * 128 : pair * 256 + part * 128 + 128,
                        ]
                        total = piece if total is None else total + piece
                holder[pair * plane2 : (pair + 1) * plane2, tile * 128 : (tile + 1) * 128] = total
    down = contract_fine(back3[...], even3[...])
    down = pltpu.roll(down, down.shape[1] - c2, 1) + contract_fine(back3[...], odd3[...])
    for l in range(length2):
        rows2[l * plane2 : (l + 1) * plane2, :] = down[:, l * c2 : (l + 1) * c2]
    slope2 = half(rows2[...]).astype(f32) * slope_of(pre2)
    delta2 = half(slope2)
    for chunk in late:
        chunk.scatter()
    grad2 = contract(half(slope2.T), p2[...])
    g2[...] = jnp.zeros_like(g2)
    for pair in range(9):
        g2[:, pair * 3 * c1 : (pair + 1) * 3 * c1] = grad2[:, pair * 128 : pair * 128 + 3 * c1]

    spread2 = contract(delta2, w2p[...])
    for pair in range(9):
        for l in range(length2):
            holder = odd2 if l % 2 else even2
            holder[pair * plane2 : (pair + 1) * plane2, (l // 2) * 128 : (l // 2 + 1) * 128] = spread2[
                l * plane2 : (l + 1) * plane2, pair * 128 : (pair + 1) * 128
            ]
    tail = jnp.zeros((plane1, 128), f32)
    left = jnp.concatenate([contract_fine(back2[...], even2[...]), tail], axis=1)
    right = jnp.concatenate([contract_fine(back2[...], odd2[...]), tail], axis=1)
    down = pltpu.roll(left, width1 + 128 - c1, 1) + pltpu.roll(right, c1, 1)
    step = BLOCK * c1
    down = jnp.concatenate([down[:, block * step : (block + 1) * step] for block in range(blocks)], axis=0)
    slope1 = down * slope_of(pre1)
    grad1 = contract(half(slope1.T), p1[...])
    tiles = []
    for pair in range(9):
        total = grad1[:c1, pair * 128 : (pair + 1) * 128]
        for l in range(1, BLOCK):
            tile = grad1[l * c1 : (l + 1) * c1, pair * 128 : (pair + 1) * 128]
            total = total + pltpu.roll(tile, 128 - 2 * l * channels, 1)
        tiles.append(half(total))
    first = contract(jnp.concatenate(tiles, axis=1), taps[...], 1)

    tiles2 = g2.shape[1] // 128
    for tile in range(tiles2):
        early_own[tile * c2 : (tile + 1) * c2, :] = half(g2[:, tile * 128 : (tile + 1) * 128])
    early_own[tiles2 * c2 : tiles2 * c2 + c1, : first.shape[1]] = half(first)
    early.begin()
    late[0].gather_plane()
    early.scatter()
    for chunk in late[1:]:
        chunk.gather_plane()
    early.gather_plane()
    for chunk in late:
        chunk.gather_line()
        chunk.spread()
    early.gather_line()
    early.spread()
    for chunk in late:
        chunk.pass_on()
    def finish(at, chunk):
        chunk.settle()
        low, high = starts[at], min(27 * c2, starts[at] + cuts[at])
        third_out[low:high, :] = chunk.whole[: high - low, :].astype(f32) * factor
    for at, chunk in enumerate(late[:-1]):
        finish(at, chunk)
    early.pass_on()
    early.settle()
    for tile in range(tiles2):
        wide = min(128, second_out.shape[1] - tile * 128)
        value = early.whole[tile * c2 : (tile + 1) * c2, :].astype(f32) * factor
        second_out[:, tile * 128 : tile * 128 + wide] = value[:, :wide]
    value = early.whole[tiles2 * c2 : tiles2 * c2 + c1, :].astype(f32) * factor
    first_out[...] = value[:, : first_out.shape[1]]
    finish(chunks - 1, late[-1])
    early.drain(everything)
    incoming.drain()


def flush_kernel(*refs):
    copies = [pltpu.make_async_copy(refs[at], refs[3 + at], refs[6].at[at]) for at in range(3)]
    for copy in copies:
        copy.start()
    for copy in copies:
        copy.wait()


def per_device(volumes, w_first, w_second, w_third, map_grad):
    slabs = lax.axis_size("slab")
    devices = lax.axis_size("vol") * slabs
    chips = devices // 2
    lines = chips // (2 * slabs)
    factor = 1.0 / (map_grad.shape[0] * devices)
    parts, channels, level, height, width = volumes.shape
    depth = level * slabs
    tables, places = tables_of(channels, depth, height, width)
    c1, c2, c3 = w_first.shape[0], w_second.shape[0], w_third.shape[0]
    plane1 = depth * height // 4
    plane2 = depth * height // 16
    length2 = width // 4
    cells = plane2 * length2
    bf16, f32 = jnp.bfloat16, jnp.float32
    planes = 2 * slabs
    tiles2 = pl.cdiv(27 * c1, 128)
    cuts = cuts_of(27 * c2, planes, SHARES)
    early_rows = chunk_rows(tiles2 * c2 + c1, planes)
    operands = (
        volumes.reshape(parts, channels, level * height, width),
        w_first,
        w_second,
        w_third.T,
        map_grad[0].transpose(1, 2, 3, 0).reshape(cells, c3),
        tables,
    )
    dma = pltpu.SemaphoreType.DMA
    scratch = [(operand.shape, operand.dtype) for operand in operands]
    scratch.append(dma((len(operands),)))
    scratch += [
        ((width // (2 * BLOCK) * plane1, 9 * 128), bf16),
        ((cells, 9 * 128), bf16),
        ((cells, 9 * 256), bf16),
        ((BLOCK * c1, 9 * 128), bf16),
        ((c2, 9 * 128), bf16),
        ((9 * 256, c3), bf16),
        ((plane2, length2 * c2), f32),
        ((9 * plane2, length2 * c2 + 128), f32),
        ((9 * plane2, length2 * c2 + 128), f32),
        ((9 * plane2, width // 2 * c1), f32),
        ((9 * plane2, width // 2 * c1), f32),
        ((cells, c2), f32),
        ((c2, tiles2 * 128), f32),
        ((slabs, level * height, channels * width), bf16),
        ((slabs, level * height, channels * width), bf16),
        dma((2,)),
        ((sum(cuts), c3), bf16),
        ((early_rows, 128), bf16),
        ((sum(Summed.sent_rows(rows, planes, lines) for rows in cuts + [early_rows]), 128), bf16),
        dma((1,)),
    ]
    kinds = [DIRECT[min(at, 1)] for at in range(len(cuts))] + [DIRECT[2]]
    for rows, kind in zip(cuts + [early_rows], kinds):
        block = rows // (2 * planes)
        for count in (planes, planes, 2 * planes, 1, lines, 2 * planes):
            scratch.append(((count * block, 128), bf16))
        scratch.append(dma((Summed.sems(*kind, planes),)))
    scratch = [pltpu.VMEM(*entry) if isinstance(entry, tuple) else entry for entry in scratch]
    in_hbm = pl.BlockSpec(memory_space=pltpu.HBM)
    in_vmem = pl.BlockSpec(memory_space=pltpu.VMEM)
    results = pl.pallas_call(
        functools.partial(step_kernel, slabs, lines, cuts, factor, places),
        out_shape=[
            pltpu.VMEM(shape, f32) for shape in (w_first.shape, w_second.shape, (27 * c2, c3))
        ],
        in_specs=[in_hbm] * len(operands),
        out_specs=[in_vmem] * 3,
        scratch_shapes=scratch,
        compiler_params=pltpu.CompilerParams(
            collective_id=0, has_side_effects=True, vmem_limit_bytes=(56) << 20
        ),
        name="step",
    )(*operands)
    first, second, third = pl.pallas_call(
        flush_kernel,
        out_shape=[jax.ShapeDtypeStruct(result.shape, f32) for result in results],
        in_specs=[in_vmem] * 3,
        out_specs=[in_hbm] * 3,
        scratch_shapes=[dma((3,))],
        compiler_params=pltpu.CompilerParams(vmem_limit_bytes=4 << 20),
        name="flush",
    )(*results)
    return first, second, third.T


def solution(mesh):
    return jax.shard_map(
        per_device,
        mesh=mesh,
        in_specs=(
            P("vol", None, "slab", None, None),
            P(),
            P(),
            P(),
            P(("vol", "slab"), None, None, None, None),
        ),
        out_specs=(P(), P(), P()),
        check_vma=False,
    )
```

```python
import functools

import jax
import jax.numpy as jnp
import numpy as np
from jax import lax
from jax.experimental import pallas as pl
from jax.experimental.pallas import tpu as pltpu
from jax.sharding import PartitionSpec as P

MESH = pl.DeviceIdType.MESH
BLOCK = 8
SHARES = (3, 5, 6)
DIRECT = ((True, False), (False, False), (False, True))


def one_hot(rows, cols, pairs):
    table = np.zeros((rows, cols), np.float32)
    for row, col in pairs:
        table[row, col] = 1.0
    return table


def cell_picks(depth, height, stride):
    out_depth, out_height = depth // stride, height // stride
    pairs = []
    for a in range(3):
        for b in range(3):
            for i in range(out_depth):
                for j in range(out_height):
                    z, y = stride * i + a - 1, stride * j + b - 1
                    if 0 <= z < depth and 0 <= y < height:
                        row = ((a * 3 + b) * out_depth + i) * out_height + j
                        pairs.append((row, z * height + y))
    return one_hot(9 * out_depth * out_height, depth * height, pairs)


def tables_of(channels, depth, height, width):
    blocks = width // (2 * BLOCK)
    spread = np.zeros((channels, width, blocks * 128), np.float32)
    for block in range(blocks):
        for at in range(2 * BLOCK + 1):
            x = 2 * BLOCK * block - 1 + at
            if x >= 0:
                for k in range(channels):
                    spread[k, x, block * 128 + at * channels + k] = 1.0
    taps = one_hot(
        27 * channels,
        9 * 128,
        [
            (pair * 3 * channels + lane, pair * 128 + lane)
            for pair in range(9)
            for lane in range(3 * channels)
        ],
    )
    plane, length = (depth // 4) * (height // 4), width // 4
    order = one_hot(
        plane * length,
        plane * length,
        [(l * plane + p, p * length + l) for l in range(length) for p in range(plane)],
    )
    second = cell_picks(depth // 2, height // 2, 2)
    third = cell_picks(depth // 4, height // 4, 1)
    spread = spread.reshape(channels * width, -1)
    tables = (spread, cell_picks(depth, height, 2), second, third, second.T, third.T, taps, order)
    return shelve(tables)


def shelve(tables):
    places, shelf, lane, height = {}, 0, 0, 0
    width = max(pl.cdiv(table.shape[1], 128) * 128 for table in tables)
    for at in sorted(range(len(tables)), key=lambda at: (-tables[at].shape[0], at)):
        rows, cols = tables[at].shape
        if lane + cols > width:
            shelf, lane, height = shelf + height, 0, 0
        places[at] = (shelf, lane, rows, cols)
        lane += pl.cdiv(cols, 128) * 128
        height = max(height, pl.cdiv(rows, 16) * 16)
    packed = np.zeros((shelf + height, width), np.float32)
    for at, (row, lane, rows, cols) in places.items():
        packed[row : row + rows, lane : lane + cols] = tables[at]
    return jnp.asarray(packed, jnp.bfloat16), [places[at] for at in range(len(tables))]


def contract(lhs, rhs, rhs_dim=0):
    return lax.dot_general(
        lhs, rhs, (((1,), (rhs_dim,)), ((), ())), preferred_element_type=jnp.float32
    )


def contract_fine(lhs, rhs):
    coarse = half(rhs)
    return contract(lhs, coarse) + contract(lhs, half(rhs - coarse.astype(jnp.float32)))


def sigmoid(pre):
    return 1.0 / (1.0 + jnp.exp(-pre))


def slope_of(pre):
    sigma = sigmoid(pre)
    return sigma * (1.0 + pre * (1.0 - sigma))


def half(value):
    return value.astype(jnp.bfloat16)


def chunk_rows(rows, planes):
    return pl.cdiv(rows, 32 * planes) * 32 * planes


def cuts_of(rows, planes, shares):
    units = chunk_rows(rows, planes) // (32 * planes)
    bounds = [units * sum(shares[:at]) // sum(shares) for at in range(len(shares) + 1)]
    return [32 * planes * (high - low) for low, high in zip(bounds, bounds[1:]) if high > low]


class Load:
    def __init__(self, sources, targets, sems):
        self.copies = [
            pltpu.make_async_copy(source, target, sems.at[index])
            for index, (source, target) in enumerate(zip(sources, targets))
        ]
        self.targets = targets

    def start(self):
        for copy in self.copies:
            copy.start()

    def get(self, index):
        self.copies[index].wait()
        return self.targets[index]


class Exchange:
    def __init__(self, source, held, sems, slabs, ring):
        self.slabs = slabs
        self.source, self.held, self.sems = source, held, sems
        self.vol, self.slab = ring.vol, ring.slab

    def copy(self, source, target, other):
        return pltpu.make_async_remote_copy(
            src_ref=source,
            dst_ref=target,
            send_sem=self.sems.at[0],
            recv_sem=self.sems.at[1],
            device_id=(self.vol, other),
            device_id_type=MESH,
        )

    def start(self):
        for step in range(1, self.slabs):
            other = lax.rem(self.slab + step, self.slabs)
            self.copy(self.source.at[other], self.held.at[self.slab], other).start()
        self.held[self.slab] = self.source[self.slab]

    def everything(self):
        other = lax.rem(self.slab + 1, self.slabs)
        rest = pl.ds(0, self.slabs - 1)
        return self.copy(self.source.at[rest], self.held.at[rest], other)

    def wait_all(self):
        self.everything().wait_recv()

    def drain(self):
        self.everything().wait_send()


class Ring:
    def __init__(self, slabs, lines):
        self.slabs, self.lines, self.planes = slabs, lines, 2 * slabs
        self.vol = lax.axis_index("vol")
        self.slab = lax.axis_index("slab")
        self.core = lax.rem(self.vol, 2)
        self.side = lax.rem(self.vol // 2, 2)
        self.at_line = self.vol // 4
        self.at_plane = self.side * slabs + self.slab
        self.half = self.core_of(self.core, self.side, self.at_line)
        self.pair = (self.vol + 1 - 2 * self.core, self.slab)

    def core_of(self, half, side, line):
        return half

    def at(self, line, plane, half):
        side = plane // self.slabs
        core = self.core_of(half, side, line)
        return ((line * 2 + side) * 2 + core, lax.rem(plane, self.slabs))

    def in_plane(self, step, flip=0):
        other = lax.rem(self.at_plane + step, self.planes)
        half = 1 - self.half if flip else self.half
        return other, self.at(self.at_line, other, half)

    def in_line(self, step):
        other = lax.rem(self.at_line + step, self.lines)
        return other, self.at(other, self.at_plane, self.half)

    def greet(self):
        barrier = pltpu.get_barrier_semaphore()
        partners = [self.in_plane(step, 0)[1] for step in range(1, self.planes)]
        partners += [self.pair]
        partners += [self.in_plane(step, 1)[1] for step in range(1, self.planes)]
        partners += [self.in_line(step)[1] for step in range(1, self.lines)]
        for partner in partners:
            pl.semaphore_signal(barrier, inc=1, device_id=partner, device_id_type=MESH)
        return lambda: pl.semaphore_wait(barrier, len(partners))


class Summed:
    OUT, LINE, ACROSS, SWAP = range(4)

    @staticmethod
    def sems(direct_out, direct, planes):
        return (3 if direct_out else 4) + (0 if direct else 1)

    @staticmethod
    def sent_rows(rows, planes, lines):
        return rows // (2 * planes) * (2 * (2 * planes - 1) + lines - 1)

    def __init__(self, ring, sent, direct_out, direct, own, from_pair, mine, landed, middle, lined, whole, sems):
        self.ring, self.direct_out, self.direct = ring, direct_out, direct
        self.own, self.from_pair, self.mine = own, from_pair, mine
        self.landed, self.middle, self.lined = landed, middle, lined
        self.whole, self.sems_at, self.sent = whole, sems, sent
        self.block = middle.shape[0]
        self.rows = ring.planes * self.block
        self.spot = ring.half * ring.planes + ring.at_plane

    def blocks(self, index, count=1):
        if isinstance(index, int):
            return pl.ds(index * self.block, count * self.block)
        return pl.ds(pl.multiple_of(index * self.block, 16), count * self.block)

    def halves(self, index):
        return pl.ds(pl.multiple_of(index * self.rows, 16), self.rows)

    def remote(self, source, target, received, device):
        return pltpu.make_async_remote_copy(
            src_ref=source,
            dst_ref=target,
            send_sem=self.sent.at[0],
            recv_sem=self.sems_at.at[received],
            device_id=device,
            device_id_type=MESH,
        )

    def await_blocks(self, ref, count, received):
        part = ref.at[self.blocks(0, count)]
        self.remote(part, part, received, self.ring.pair).wait_recv()

    def swap(self):
        source = self.own.at[self.halves(1 - self.ring.half)]
        return self.remote(source, self.from_pair, self.SWAP, self.ring.pair)

    def plane_out(self, step, flip=0):
        other, device = self.ring.in_plane(step, flip)
        slot = flip * self.ring.planes + step - 1
        if self.direct_out:
            half_at = 1 - self.ring.half if flip else self.ring.half
            source = self.own.at[self.blocks(half_at * self.ring.planes + other)]
        else:
            source = self.mine.at[self.blocks(other)]
        return self.remote(source, self.landed.at[self.blocks(slot)], self.OUT, device)

    def outs(self):
        steps = [(step, 0) for step in range(1, self.ring.planes)]
        if self.direct_out:
            steps += [(step, 1) for step in range(self.ring.planes)]
        return steps

    def line_out(self, step):
        target = self.lined.at[self.blocks(step - 1)]
        device = self.ring.in_line(step)[1]
        return self.remote(self.middle, target, self.LINE, device)

    def plane_back(self, step):
        block = self.whole.at[self.blocks(self.spot)]
        received = self.ACROSS if self.direct else (3 if self.direct_out else 4)
        return self.remote(block, block, received, self.ring.in_plane(step)[1])

    def across(self, step):
        planes = self.ring.planes
        if self.direct:
            source, device = self.ring.at_plane, self.ring.in_plane(step, 1)[1]
        else:
            source, device = lax.rem(self.ring.at_plane - step + planes, planes), self.ring.pair
        block = self.whole.at[self.blocks(self.ring.half * planes + source)]
        return self.remote(block, block, self.ACROSS, device)

    def begin(self):
        if self.direct_out:
            for step, flip in self.outs():
                self.plane_out(step, flip).start()
        else:
            self.swap().start()

    def scatter(self):
        if self.direct_out:
            return
        self.swap().wait_recv()
        own = self.own[self.halves(self.ring.half), :].astype(jnp.float32)
        self.mine[...] = half(own + self.from_pair[...].astype(jnp.float32))
        for step, flip in self.outs():
            self.plane_out(step, flip).start()

    def gather_plane(self):
        if self.direct_out:
            running = self.own[self.blocks(self.spot), :].astype(jnp.float32)
        else:
            running = self.mine[self.blocks(self.ring.at_plane), :].astype(jnp.float32)
        count = len(self.outs())
        self.await_blocks(self.landed, count, self.OUT)
        for slot in range(count):
            running = running + self.landed[self.blocks(slot), :].astype(jnp.float32)
        self.middle[...] = half(running)
        self.lined[self.blocks(self.ring.lines - 1), :] = self.middle[...]
        for step in range(1, self.ring.lines):
            self.line_out(step).start()

    def gather_line(self):
        self.await_blocks(self.lined, self.ring.lines - 1, self.LINE)
        line, lines = self.ring.at_line, self.ring.lines
        running = None
        for source in range(lines):
            slot = lax.rem(line - source + lines - 1, lines)
            value = self.lined[self.blocks(slot), :].astype(jnp.float32)
            running = value if running is None else running + value
        self.whole[self.blocks(self.spot), :] = half(running)

    def spread(self):
        for step in range(1, self.ring.planes):
            self.plane_back(step).start()
            if self.direct:
                self.across(step).start()
        self.across(0).start()

    def pass_on(self):
        if self.direct:
            return
        back = 3 if self.direct_out else 4
        self.await_blocks(self.landed, self.ring.planes - 1, back)
        for step in range(1, self.ring.planes):
            self.across(step).start()

    def settle(self):
        planes = self.ring.planes
        self.await_blocks(self.landed, 2 * planes - 1 if self.direct else planes, self.ACROSS)

    def drain(self, everything):
        self.remote(everything, everything, self.OUT, self.ring.pair).wait_send()


def step_kernel(slabs, lines, cuts, factor, places, *refs):
    chunks = len(cuts)
    starts = [sum(cuts[:at]) for at in range(chunks)]
    sources, refs = refs[:6], refs[6:]
    (first_out, second_out, third_out), refs = refs[:3], refs[3:]
    loaded, load_sems, refs = refs[:6], refs[6], refs[7:]
    (p1, p2, p3, w1b, w2p, w3p, a2, even3, odd3, even2, odd2, rows2, g2), refs = refs[:13], refs[13:]
    outgoing, vol, vol_sems, late_own, early_own, everything, sent, *parts = refs
    ring = Ring(slabs, lines)
    load = Load(sources, loaded, load_sems)
    load.copies[0].start()
    ready = ring.greet()
    for copy in load.copies[1:]:
        copy.start()
    late = [
        Summed(ring, sent, *DIRECT[min(at, 1)], late_own.at[pl.ds(starts[at], cuts[at])], *parts[7 * at : 7 * at + 7])
        for at in range(chunks)
    ]
    early = Summed(ring, sent, *DIRECT[2], early_own, *parts[7 * chunks :])

    raw = load.get(0)
    for part in range(slabs):
        outgoing[part] = jnp.concatenate([raw[part, k] for k in range(raw.shape[1])], axis=1)
    ready()
    incoming = Exchange(outgoing, vol, vol_sems, slabs, ring)
    incoming.start()

    f32 = jnp.float32
    channels = raw.shape[1]
    w1, w2, w3, mg = load.get(1), load.get(2), load.get(3), load.get(4)
    packed = load.get(5)
    spread, pick1, pick2, pick3, back2, back3, taps, order = [
        packed.at[row : row + rows, lane : lane + cols] for row, lane, rows, cols in places
    ]
    c1, c2, c3 = w1.shape[0], w2.shape[0], w3.shape[1]
    blocks = spread.shape[1] // 128
    plane1, plane2 = pick1.shape[0] // 9, pick2.shape[0] // 9
    length2 = mg.shape[0] // plane2
    width1 = blocks * BLOCK * c1
    width2 = length2 * c2

    wide = contract(w1[...], taps[...])
    for pair in range(9):
        tile = wide[:, pair * 128 : (pair + 1) * 128]
        for l in range(BLOCK):
            moved = pltpu.roll(tile, 2 * l * channels, 1) if l else tile
            w1b[l * c1 : (l + 1) * c1, pair * 128 : (pair + 1) * 128] = half(moved)
    w2p[...] = jnp.zeros_like(w2p)
    w3p[...] = jnp.zeros_like(w3p)
    for pair in range(9):
        w2p[:, pair * 128 : pair * 128 + 3 * c1] = w2[:, pair * 3 * c1 : (pair + 1) * 3 * c1]
        w3p[pair * 256 : pair * 256 + 3 * c2, :] = w3[pair * 3 * c2 : (pair + 1) * 3 * c2, :]

    given = contract(order[...], mg[...])
    late_own[27 * c2 :, :] = jnp.zeros((late_own.shape[0] - 27 * c2, c3), jnp.bfloat16)
    early_own[...] = jnp.zeros_like(early_own)
    incoming.wait_all()
    levels = [half(contract(vol[part], spread[...])) for part in range(slabs)]
    r1 = half(contract(pick1[...], jnp.concatenate(levels, axis=0)))
    for pair in range(9):
        for block in range(blocks):
            p1[block * plane1 : (block + 1) * plane1, pair * 128 : (pair + 1) * 128] = r1[
                pair * plane1 : (pair + 1) * plane1, block * 128 : (block + 1) * 128
            ]
    pre1 = contract(p1[...], w1b[...], 1)
    act1 = half(pre1 * sigmoid(pre1))
    a1 = jnp.concatenate(
        [act1[block * plane1 : (block + 1) * plane1, :] for block in range(blocks)], axis=1
    )
    r2 = contract(pick2[...], a1)
    r2 = jnp.concatenate([r2, jnp.zeros((9 * plane2, 128), f32)], axis=1)
    sides = (half(pltpu.roll(r2, c1, 1)), half(pltpu.roll(r2, width1 + 128 - c1, 1)))
    for l in range(length2):
        chunk = sides[l % 2][:, (l // 2) * 128 : (l // 2 + 1) * 128]
        for pair in range(9):
            p2[l * plane2 : (l + 1) * plane2, pair * 128 : (pair + 1) * 128] = chunk[
                pair * plane2 : (pair + 1) * plane2, :
            ]
    pre2 = contract(p2[...], w2p[...], 1)
    act2 = pre2 * sigmoid(pre2)
    for l in range(length2):
        a2[:, l * c2 : (l + 1) * c2] = act2[l * plane2 : (l + 1) * plane2, :]
    r3 = contract(pick3[...], half(a2[...]))
    r3 = jnp.concatenate([r3, jnp.zeros((9 * plane2, 256), f32)], axis=1)
    sides = (half(pltpu.roll(r3, c2, 1)), half(r3))
    for l in range(length2):
        chunk = sides[l % 2][:, (l // 2) * 128 : (l // 2) * 128 + 256]
        for pair in range(9):
            p3[l * plane2 : (l + 1) * plane2, pair * 256 : (pair + 1) * 256] = chunk[
                pair * plane2 : (pair + 1) * plane2, :
            ]
    pre3 = contract(p3[...], w3p[...])
    slope3 = given * slope_of(pre3)
    delta3 = half(slope3)
    grad3 = contract(delta3.T, p3[...])
    for pair in range(9):
        for lane in range(0, 3 * c2, 128):
            wide = min(128, 3 * c2 - lane)
            turned = half(grad3[:, pair * 256 + lane : pair * 256 + lane + 128]).T
            at = pair * 3 * c2 + lane
            begun = [chunk for chunk in range(chunks - 1) if at < starts[chunk] + cuts[chunk] <= at + wide]
            late_own[at : at + wide, :] = turned[:wide, :]
            for chunk in begun:
                late[chunk].begin()
    late[-1].begin()

    spread3 = contract(delta3, w3p[...], 1)
    for pair in range(9):
        for side, holder in ((0, even3), (1, odd3)):
            for tile in range(length2 // 2 + 1):
                total = None
                for part in range(2):
                    l = 2 * (tile - part) + side
                    if 0 <= l < length2:
                        piece = spread3[
                            l * plane2 : (l + 1) * plane2,
                            pair * 256 + part * 128 : pair * 256 + part * 128 + 128,
                        ]
                        total = piece if total is None else total + piece
                holder[pair * plane2 : (pair + 1) * plane2, tile * 128 : (tile + 1) * 128] = total
    down = contract_fine(back3[...], even3[...])
    down = pltpu.roll(down, down.shape[1] - c2, 1) + contract_fine(back3[...], odd3[...])
    for l in range(length2):
        rows2[l * plane2 : (l + 1) * plane2, :] = down[:, l * c2 : (l + 1) * c2]
    slope2 = half(rows2[...]).astype(f32) * slope_of(pre2)
    delta2 = half(slope2)
    for chunk in late:
        chunk.scatter()
    grad2 = contract(half(slope2.T), p2[...])
    g2[...] = jnp.zeros_like(g2)
    for pair in range(9):
        g2[:, pair * 3 * c1 : (pair + 1) * 3 * c1] = grad2[:, pair * 128 : pair * 128 + 3 * c1]

    spread2 = contract(delta2, w2p[...])
    for pair in range(9):
        for l in range(length2):
            holder = odd2 if l % 2 else even2
            holder[pair * plane2 : (pair + 1) * plane2, (l // 2) * 128 : (l // 2 + 1) * 128] = spread2[
                l * plane2 : (l + 1) * plane2, pair * 128 : (pair + 1) * 128
            ]
    tail = jnp.zeros((plane1, 128), f32)
    left = jnp.concatenate([contract_fine(back2[...], even2[...]), tail], axis=1)
    right = jnp.concatenate([contract_fine(back2[...], odd2[...]), tail], axis=1)
    down = pltpu.roll(left, width1 + 128 - c1, 1) + pltpu.roll(right, c1, 1)
    step = BLOCK * c1
    down = jnp.concatenate([down[:, block * step : (block + 1) * step] for block in range(blocks)], axis=0)
    slope1 = down * slope_of(pre1)
    grad1 = contract(half(slope1.T), p1[...])
    tiles = []
    for pair in range(9):
        total = grad1[:c1, pair * 128 : (pair + 1) * 128]
        for l in range(1, BLOCK):
            tile = grad1[l * c1 : (l + 1) * c1, pair * 128 : (pair + 1) * 128]
            total = total + pltpu.roll(tile, 128 - 2 * l * channels, 1)
        tiles.append(half(total))
    first = contract(jnp.concatenate(tiles, axis=1), taps[...], 1)

    tiles2 = g2.shape[1] // 128
    for tile in range(tiles2):
        early_own[tile * c2 : (tile + 1) * c2, :] = half(g2[:, tile * 128 : (tile + 1) * 128])
    early_own[tiles2 * c2 : tiles2 * c2 + c1, : first.shape[1]] = half(first)
    early.begin()
    late[0].gather_plane()
    early.scatter()
    for chunk in late[1:]:
        chunk.gather_plane()
    early.gather_plane()
    for chunk in late:
        chunk.gather_line()
        chunk.spread()
    early.gather_line()
    early.spread()
    for chunk in late:
        chunk.pass_on()
    def finish(at, chunk):
        chunk.settle()
        low, high = starts[at], min(27 * c2, starts[at] + cuts[at])
        third_out[low:high, :] = chunk.whole[: high - low, :].astype(f32) * factor
    for at, chunk in enumerate(late[:-1]):
        finish(at, chunk)
    early.pass_on()
    early.settle()
    for tile in range(tiles2):
        wide = min(128, second_out.shape[1] - tile * 128)
        value = early.whole[tile * c2 : (tile + 1) * c2, :].astype(f32) * factor
        second_out[:, tile * 128 : tile * 128 + wide] = value[:, :wide]
    value = early.whole[tiles2 * c2 : tiles2 * c2 + c1, :].astype(f32) * factor
    first_out[...] = value[:, : first_out.shape[1]]
    finish(chunks - 1, late[-1])
    early.drain(everything)
    incoming.drain()


def flush_kernel(*refs):
    copies = [pltpu.make_async_copy(refs[at], refs[3 + at], refs[6].at[at]) for at in range(3)]
    for copy in copies:
        copy.start()
    for copy in copies:
        copy.wait()


def per_device(volumes, w_first, w_second, w_third, map_grad):
    slabs = lax.axis_size("slab")
    devices = lax.axis_size("vol") * slabs
    chips = devices // 2
    lines = chips // (2 * slabs)
    factor = 1.0 / (map_grad.shape[0] * devices)
    parts, channels, level, height, width = volumes.shape
    depth = level * slabs
    tables, places = tables_of(channels, depth, height, width)
    c1, c2, c3 = w_first.shape[0], w_second.shape[0], w_third.shape[0]
    plane1 = depth * height // 4
    plane2 = depth * height // 16
    length2 = width // 4
    cells = plane2 * length2
    bf16, f32 = jnp.bfloat16, jnp.float32
    planes = 2 * slabs
    tiles2 = pl.cdiv(27 * c1, 128)
    cuts = cuts_of(27 * c2, planes, SHARES)
    early_rows = chunk_rows(tiles2 * c2 + c1, planes)
    operands = (
        volumes.reshape(parts, channels, level * height, width),
        w_first,
        w_second,
        w_third.T,
        map_grad[0].transpose(1, 2, 3, 0).reshape(cells, c3),
        tables,
    )
    dma = pltpu.SemaphoreType.DMA
    scratch = [(operand.shape, operand.dtype) for operand in operands]
    scratch.append(dma((len(operands),)))
    scratch += [
        ((width // (2 * BLOCK) * plane1, 9 * 128), bf16),
        ((cells, 9 * 128), bf16),
        ((cells, 9 * 256), bf16),
        ((BLOCK * c1, 9 * 128), bf16),
        ((c2, 9 * 128), bf16),
        ((9 * 256, c3), bf16),
        ((plane2, length2 * c2), f32),
        ((9 * plane2, length2 * c2 + 128), f32),
        ((9 * plane2, length2 * c2 + 128), f32),
        ((9 * plane2, width // 2 * c1), f32),
        ((9 * plane2, width // 2 * c1), f32),
        ((cells, c2), f32),
        ((c2, tiles2 * 128), f32),
        ((slabs, level * height, channels * width), bf16),
        ((slabs, level * height, channels * width), bf16),
        dma((2,)),
        ((sum(cuts), c3), bf16),
        ((early_rows, 128), bf16),
        ((sum(Summed.sent_rows(rows, planes, lines) for rows in cuts + [early_rows]), 128), bf16),
        dma((1,)),
    ]
    kinds = [DIRECT[min(at, 1)] for at in range(len(cuts))] + [DIRECT[2]]
    for rows, kind in zip(cuts + [early_rows], kinds):
        block = rows // (2 * planes)
        for count in (planes, planes, 2 * planes, 1, lines, 2 * planes):
            scratch.append(((count * block, 128), bf16))
        scratch.append(dma((Summed.sems(*kind, planes),)))
    scratch = [pltpu.VMEM(*entry) if isinstance(entry, tuple) else entry for entry in scratch]
    in_hbm = pl.BlockSpec(memory_space=pltpu.HBM)
    in_vmem = pl.BlockSpec(memory_space=pltpu.VMEM)
    results = pl.pallas_call(
        functools.partial(step_kernel, slabs, lines, cuts, factor, places),
        out_shape=[
            pltpu.VMEM(shape, f32) for shape in (w_first.shape, w_second.shape, (27 * c2, c3))
        ],
        in_specs=[in_hbm] * len(operands),
        out_specs=[in_vmem] * 3,
        scratch_shapes=scratch,
        compiler_params=pltpu.CompilerParams(
            collective_id=0, has_side_effects=True, vmem_limit_bytes=(56) << 20
        ),
        name="step",
    )(*operands)
    first, second, third = pl.pallas_call(
        flush_kernel,
        out_shape=[jax.ShapeDtypeStruct(result.shape, f32) for result in results],
        in_specs=[in_vmem] * 3,
        out_specs=[in_hbm] * 3,
        scratch_shapes=[dma((3,))],
        compiler_params=pltpu.CompilerParams(vmem_limit_bytes=4 << 20),
        name="flush",
    )(*results)
    return first, second, third.T


def solution(mesh):
    return jax.shard_map(
        per_device,
        mesh=mesh,
        in_specs=(
            P("vol", None, "slab", None, None),
            P(),
            P(),
            P(),
            P(("vol", "slab"), None, None, None, None),
        ),
        out_specs=(P(), P(), P()),
        check_vma=False,
    )
```
